128 devices in a mesh: gx: 16 (over z, y), gz: 8 (over x, core).
Axes of the slice: x: 4, y: 4, z: 4, core: 2. Of those that a mesh axis runs over, the one named last changes fastest.
Arguments:
- density: float32 [1024, 128, 128], P('gx', 'gz'), may hold values from 1 to 2
- momentum: float32 [3, 1024, 128, 128], P(None, 'gx', 'gz'), may hold values from -1 to 1
- energy: float32 [1024, 128, 128], P('gx', 'gz'), may hold values from 4 to 6
- metric: float32 [1024, 128, 128], P('gx', 'gz'), may hold values from 0.5 to 1.5
- deriv_matrix: float32 [1024, 1024], replicated, may hold values from -0.1875 to 0.1875
- smooth_matrix: float32 [1024, 1024], replicated, may hold values from -0.046875 to 0.046875
- panel_of_cell: int32 [1024, 128], P('gx', 'gz'), may hold values from 0 to 63, as said below
- shape_index: int32 [1024, 128], P('gx', 'gz'), may hold values from 0 to 255
- mode_table: float32 [256, 128], replicated, may hold values from -0.375 to 0.375
Outputs:
- new_density: float32 [1024, 128, 128], P('gx', 'gz')
- new_momentum: float32 [3, 1024, 128, 128], P(None, 'gx', 'gz')
- new_energy: float32 [1024, 128, 128], P('gx', 'gz')
- panel_forces: float32 [64, 128], P('gx')
The draws below stay inside these ranges and needn't reach their ends.
Inputs may be any that keep to these rules, and one draw needn't show every extreme that they name: `panel_of_cell`: each of the 64 panels is one of 8 contiguous uneven runs of streamwise cells times one of 8 contiguous uneven runs of spanwise cells, panel number = run across the span * 8 + run along the stream; every panel has cells.
All inputs are finite; a program needn't handle non-finite values.
Results may differ from the reference program's by a relative error of at most 0.0003.
Values sent between devices are 32-bit elements; how exact they have to be, the bound alone decides.
No kernel may reach another device: no remote copies, remote signals or barrier semaphores. Data moves between devices by JAX's collectives and lax.ppermute only.
A program may use at most 128 MiB of HBM per device.

```python
import jax
import jax.numpy as jnp
from jax import lax

NX = 1024
NY = 128
NPX = 8
NPZ = 8
MODES = 128
NSHAPE = 256
NP = 64
NZ = 128


def run_index(key, total, blocks):
    base = total // blocks
    half = base // 2
    delta = jax.random.randint(key, (blocks // 2,), -half, half + 1)
    widths = jnp.stack([base + delta, base - delta], axis=1).reshape(-1)
    ends = jnp.cumsum(widths)
    places = jnp.arange(total)
    return jnp.sum((places[:, None] >= ends[None, :]).astype(jnp.int32), axis=1)


def draw_panel_of_cell(key, part):
    key_x = jax.random.fold_in(key, 11)
    key_z = jax.random.fold_in(key, 23)
    run_x = run_index(key_x, NX, NPX)
    run_z = run_index(key_z, NZ, NPZ)
    return (run_z[None, :] * NPX + run_x[:, None]).astype(jnp.int32)


def set_ends(result, stream_key, low, largest):
    longest = result.shape.index(max(result.shape))
    spots = []
    for shift in (0, 1):
        where = [jax.random.randint(jax.random.fold_in(stream_key, axis), (), 0, length) for axis, length in enumerate(result.shape)]
        where[longest] = (where[longest] + shift) % result.shape[longest]
        spots.append(tuple(where))
    return result.at[spots[0]].set(low).at[spots[1]].set(largest)


def levels(rng, shape, shards, smallest, largest):
    loudness = 1.0
    for axis_at, shards_of in shards:
        draws = jax.random.uniform(jax.random.fold_in(jax.random.fold_in(rng, 6), axis_at), (shards_of,), jnp.float32, smallest / len(shards), largest / len(shards))
        loudness = loudness * jnp.repeat(jnp.exp(draws), shape[axis_at] // shards_of).reshape((-1,) + (1,) * (len(shape) - 1 - axis_at))
    return loudness


def scatter_about(rng, shape, deviation, most, shards=(), dtype=jnp.bfloat16):
    entries = deviation * jax.random.normal(rng, shape, jnp.float32)
    if shards:
        entries = entries * levels(rng, shape, shards, -0.22, 0.18)
    return jnp.clip(entries, -most, most).astype(dtype)


def setup_inputs(seed: int = 0) -> dict:
    seeds = jax.random.split(jax.random.key(seed), 10)
    return {
        "density": jnp.clip(1.0 + 1.0 * jax.random.uniform(seeds[0], (NX, NZ, NY), jnp.float32) ** levels(seeds[0], (NX, NZ, NY), ((0, 16), (1, 8)), -0.2, 0.2), 1.0, 2.0),
        "momentum": scatter_about(seeds[1], (3, NX, NZ, NY), 0.3, 1.0, ((1, 16), (2, 8)), jnp.float32),
        "energy": jnp.clip(4.0 + 2.0 * jax.random.uniform(seeds[2], (NX, NZ, NY), jnp.float32) ** levels(seeds[2], (NX, NZ, NY), ((0, 16), (1, 8)), -0.2, 0.2), 4.0, 6.0),
        "metric": jnp.clip(0.5 + 1.0 * jax.random.uniform(seeds[3], (NX, NZ, NY), jnp.float32) ** levels(seeds[3], (NX, NZ, NY), ((0, 16), (1, 8)), -0.2, 0.2), 0.5, 1.5),
        "deriv_matrix": scatter_about(seeds[4], (NX, NX), NX ** -0.5, 0.1875, (), jnp.float32),
        "smooth_matrix": scatter_about(seeds[5], (NX, NX), (16 * NX) ** -0.5, 0.046875, (), jnp.float32),
        "panel_of_cell": draw_panel_of_cell(jax.random.fold_in(seeds[9], 71), 0),
        "shape_index": set_ends(jax.random.randint(seeds[7], (NX, NZ), 0, NSHAPE), jax.random.fold_in(seeds[7], 1), 0, NSHAPE - 1).astype(jnp.int32),
        "mode_table": scatter_about(seeds[8], (NSHAPE, MODES), NSHAPE ** -0.5, 0.375, (), jnp.float32),
    }


time_step = 0.05
gas_factor = 0.4
pressure_ref = 2.0


def pressure_of(state):
    kinetic = 0.5 * (state[1] * state[1] + state[2] * state[2] + state[3] * state[3]) / state[0]
    return gas_factor * (state[4] - kinetic)


def fluxes(state, direction):
    pressure = pressure_of(state)
    speed = state[1 + direction] / state[0]
    parts = [state[1 + direction]]
    for component in range(3):
        term = state[1 + component] * speed
        if component == direction:
            term = term + pressure
        parts.append(term)
    parts.append((state[4] + pressure) * speed)
    return jnp.stack(parts)


def along_y(field):
    padded = jnp.pad(field, ((0, 0), (0, 0), (0, 0), (2, 2)))
    return (8.0 * (padded[..., 3:-1] - padded[..., 1:-3]) - (padded[..., 4:] - padded[..., :-4])) / 12.0


def along_z(padded):
    return (8.0 * (padded[:, :, 3:-1] - padded[:, :, 1:-3]) - (padded[:, :, 4:] - padded[:, :, :-4])) / 12.0


def x_terms(state, deriv_matrix, smooth_matrix):
    flux = fluxes(state, 0)
    smooth = jnp.einsum('ij,kjzy->kizy', smooth_matrix, state, precision=lax.Precision.HIGHEST)
    slope = jnp.einsum('ij,kjzy->kizy', deriv_matrix, flux, precision=lax.Precision.HIGHEST)
    return smooth - slope


def rate(state, metric, deriv_matrix, smooth_matrix):
    padded = jnp.pad(fluxes(state, 2), ((0, 0), (0, 0), (2, 2), (0, 0)), mode="wrap")
    total = x_terms(state, deriv_matrix, smooth_matrix) - along_y(fluxes(state, 1)) - along_z(padded)
    return metric * total


def reference(density, momentum, energy, metric, deriv_matrix, smooth_matrix, panel_of_cell, shape_index, mode_table):
    state = jnp.concatenate([density[None], momentum, energy[None]], axis=0)
    first = state + time_step * rate(state, metric, deriv_matrix, smooth_matrix)
    final = 0.5 * state + 0.5 * (first + time_step * rate(first, metric, deriv_matrix, smooth_matrix))
    load = (pressure_of(final[:, :, :, 0]) - pressure_ref) * metric[:, :, 0]
    keys = (panel_of_cell * NSHAPE + shape_index).reshape(-1).astype(jnp.int32)
    summed = jax.ops.segment_sum(load.reshape(-1), keys, num_segments=NP * NSHAPE).reshape(NP, NSHAPE)
    forces = jnp.dot(summed, mode_table, precision=lax.Precision.HIGHEST)
    return final[0], final[1:4], final[4], forces
```

```python
import functools

import jax
import jax.numpy as jnp
from jax import lax
from jax.experimental import pallas as pl
from jax.experimental.pallas import tpu as pltpu
from jax.sharding import PartitionSpec as P

NP = 64
NSHAPE = 256
XB = 64
ZB = 16
YB = 8
LANES = 128
HALF = 64

time_step = 0.05
gas_factor = 0.4
pressure_ref = 2.0
middle = (1.5, 0.0, 0.0, 0.0, 5.0)
near = 8.0 / 12.0
far = 1.0 / 12.0

f32 = jnp.float32
bf16 = jnp.bfloat16


def params():
    return pltpu.CompilerParams()


def cost(flops, nbytes):
    return pl.CostEstimate(flops=flops, bytes_accessed=nbytes, transcendentals=0)


def pressure_of(q, inverse):
    return gas_factor * (q[4] - 0.5 * (q[1] * q[1] + q[2] * q[2] + q[3] * q[3]) * inverse)


def flux(q, pressure, inverse, direction):
    speed = q[1 + direction] * inverse
    parts = [q[1 + direction]]
    for component in range(3):
        term = q[1 + component] * speed
        if component == direction:
            term = term + pressure
        parts.append(term)
    parts.append((q[4] + pressure) * speed)
    return parts


def pack_kernel(d_ref, m_ref, e_ref, g_ref, panel_ref, shape_ref, out_ref, code_ref):
    for zp in range(8):
        for f in range(6):
            if f == 0:
                src = d_ref
            elif f < 4:
                src = m_ref.at[f - 1]
            elif f == 4:
                src = e_ref
            else:
                src = g_ref
            low = src[pl.ds(zp, XB, stride=ZB), :]
            high = src[pl.ds(zp + 8, XB, stride=ZB), :]
            tile = jnp.concatenate([low, high], axis=0).T
            out_ref[:, f * 8 + zp] = tile.reshape(16, YB, LANES)
    turned = (panel_ref[...] * NSHAPE + shape_ref[...]).astype(f32)
    code_ref[:, 0:HALF] = turned[0:8]
    code_ref[:, HALF:LANES] = turned[8:16]
    code = code_ref[...]
    for peer in range(16):
        out_ref[peer, 48] = code


def pack(density, momentum, energy, metric, panels, shapes):
    vm = pl.BlockSpec(memory_space=pltpu.VMEM)
    return pl.pallas_call(
        pack_kernel,
        out_shape=jax.ShapeDtypeStruct((16, 49, YB, LANES), f32),
        in_specs=[vm] * 6,
        out_specs=vm,
        scratch_shapes=[pltpu.VMEM((8, LANES), f32)],
        compiler_params=params(),
        cost_estimate=cost(1000000, 6400000),
        name="pack",
    )(
        density.reshape(XB * ZB, LANES),
        momentum.reshape(3, XB * ZB, LANES),
        energy.reshape(XB * ZB, LANES),
        metric.reshape(XB * ZB, LANES),
        panels.T,
        shapes.T,
    )


def emit_operands(q, q_ref, fhi_ref, flo_ref, ytop_ref, ybot_ref, ztop_ref, zbot_ref):
    inverse = 1.0 / q[0]
    pressure = pressure_of(q, inverse)
    stream = flux(q, pressure, inverse, 0)
    for f in range(5):
        rows = pl.ds(f * 128, 128)
        q_ref[rows, :] = (q[f] - middle[f]).reshape(128, LANES).astype(bf16)
        value = stream[f].reshape(128, LANES)
        high = value.astype(bf16)
        fhi_ref[rows, :] = high
        flo_ref[rows, :] = (value - high.astype(f32)).astype(bf16)
    row = lax.broadcasted_iota(jnp.int32, (YB, LANES), 0)
    normal = flux(q, pressure, inverse, 1)
    for f in range(5):
        for zq in range(4):
            top = normal[f][zq * 4]
            bot = normal[f][zq * 4]
            top = pltpu.roll(top, 2, 0)
            for z4 in range(1, 4):
                plane = normal[f][zq * 4 + z4]
                mine = (row >= 2 * z4) & (row < 2 * z4 + 2)
                shift = (2 * z4 + 2) % 8
                top = jnp.where(mine, pltpu.roll(plane, shift, 0) if shift else plane, top)
                bot = jnp.where(mine, pltpu.roll(plane, 2 * z4, 0), bot)
            ytop_ref[f, zq] = top
            ybot_ref[f, zq] = bot
    low = [q[f][0:2] for f in range(5)]
    high = [q[f][14:16] for f in range(5)]
    zlow = flux(low, pressure[0:2], inverse[0:2], 2)
    zhigh = flux(high, pressure[14:16], inverse[14:16], 2)
    for f in range(5):
        zbot_ref[f] = zlow[f]
        ztop_ref[f] = zhigh[f]


operand_shapes = [
    jax.ShapeDtypeStruct((640, 1024), bf16),
    jax.ShapeDtypeStruct((640, 1024), bf16),
    jax.ShapeDtypeStruct((640, 1024), bf16),
    jax.ShapeDtypeStruct((5, 4, YB, 1024), f32),
    jax.ShapeDtypeStruct((5, 4, YB, 1024), f32),
    jax.ShapeDtypeStruct((5, 2, YB, 1024), f32),
    jax.ShapeDtypeStruct((5, 2, YB, 1024), f32),
]
flat_spec = pl.BlockSpec((640, LANES), lambda s: (0, s))
yedge_spec = pl.BlockSpec((5, 4, YB, LANES), lambda s: (0, 0, 0, s))
zedge_spec = pl.BlockSpec((5, 2, YB, LANES), lambda s: (0, 0, 0, s))
operand_specs = [flat_spec] * 3 + [yedge_spec] * 2 + [zedge_spec] * 2
line_spec = pl.BlockSpec((5, ZB, YB, LANES), lambda s: (0, 0, 0, s))
cell_spec = pl.BlockSpec((ZB, YB, LANES), lambda s: (0, 0, s))
code_spec = pl.BlockSpec((ZB, LANES), lambda s: (0, s))


def join(a, b):
    lane = lax.broadcasted_iota(jnp.int32, a.shape, a.ndim - 1)
    axis = a.ndim - 1
    low = jnp.where(lane < HALF, a, pltpu.roll(b, HALF, axis))
    high = jnp.where(lane < HALF, pltpu.roll(a, HALF, axis), b)
    return jnp.concatenate([low, high], axis=0)


def unpack_kernel(in_ref, line_ref, metric_ref, code_ref, *operands):
    q = []
    for f in range(5):
        field = join(in_ref[0, f * 8 : f * 8 + 8], in_ref[1, f * 8 : f * 8 + 8])
        line_ref[f] = field
        q.append(field)
    metric_ref[...] = join(in_ref[0, 40:48], in_ref[1, 40:48])
    code_ref[...] = join(in_ref[0, 48], in_ref[1, 48])
    emit_operands(q, *operands)


def unpack(packed):
    return pl.pallas_call(
        unpack_kernel,
        grid=(8,),
        out_shape=[
            jax.ShapeDtypeStruct((5, ZB, YB, 1024), f32),
            jax.ShapeDtypeStruct((ZB, YB, 1024), f32),
            jax.ShapeDtypeStruct((ZB, 1024), f32),
            *operand_shapes,
        ],
        in_specs=[pl.BlockSpec((2, 49, YB, LANES), lambda s: (s, 0, 0, 0))],
        out_specs=[line_spec, cell_spec, code_spec, *operand_specs],
        compiler_params=params(),
        cost_estimate=cost(10000000, 12000000),
        name="unpack",
    )(packed)


def lines_kernel(q_ref, fhi_ref, flo_ref, smooth_ref, dhi_ref, dlo_ref, sums_ref, out_ref):
    dot = functools.partial(jnp.dot, preferred_element_type=f32)
    fhi = fhi_ref[...]
    slope = dot(fhi, dhi_ref[...]) + dot(flo_ref[...], dhi_ref[...]) + dot(fhi, dlo_ref[...])
    total = dot(q_ref[...], smooth_ref[...]) - slope
    sums = sums_ref[...]
    for f in range(5):
        rows = slice(f * 128, f * 128 + 128)
        part = total[rows]
        out_ref[rows, :] = part + middle[f] * sums if middle[f] else part


def lines(q, fhi, flo, smooth, dhi, dlo, sums):
    wide = 256
    whole = pl.BlockSpec((640, 1024), lambda n: (0, 0))
    part = pl.BlockSpec((1024, wide), lambda n: (0, n))
    out = pl.pallas_call(
        lines_kernel,
        grid=(1024 // wide,),
        out_shape=jax.ShapeDtypeStruct((640, 1024), f32),
        in_specs=[whole] * 3 + [part] * 3 + [pl.BlockSpec((1, wide), lambda n: (0, n))],
        out_specs=pl.BlockSpec((640, wide), lambda n: (0, n)),
        compiler_params=params(),
        cost_estimate=cost(8 * 640 * 1024 * 1024, 14000000),
        name="lines",
    )(q, fhi, flo, smooth, dhi, dlo, sums)
    return out.reshape(5, ZB, YB, 1024)


def slopes(q, ylo_ref, yhi_ref, zlo_ref, zhi_ref):
    inverse = 1.0 / q[0]
    pressure = pressure_of(q, inverse)
    normal = flux(q, pressure, inverse, 1)
    span = flux(q, pressure, inverse, 2)
    row = lax.broadcasted_iota(jnp.int32, (YB, LANES), 0)
    result = []
    for f in range(5):
        planes = [zlo_ref[f, 0], zlo_ref[f, 1]]
        planes += [span[f][z] for z in range(ZB)]
        planes += [zhi_ref[f, 0], zhi_ref[f, 1]]
        rows = []
        for z in range(ZB):
            g = normal[f][z]
            zq, z4 = z // 4, z % 4
            below = ylo_ref[f, zq]
            above = yhi_ref[f, zq]

            def turn(v, shift):
                shift = shift % 8
                return pltpu.roll(v, shift, 0) if shift else v

            back1 = jnp.where(row < 1, turn(below, -2 * z4 - 1), turn(g, 1))
            back2 = jnp.where(row < 2, turn(below, -2 * z4), turn(g, 2))
            ahead1 = jnp.where(row > 6, turn(above, 7 - 2 * z4), turn(g, -1))
            ahead2 = jnp.where(row > 5, turn(above, 6 - 2 * z4), turn(g, -2))
            slope_y = near * (ahead1 - back1) - far * (ahead2 - back2)
            slope_z = near * (planes[z + 3] - planes[z + 1]) - far * (planes[z + 4] - planes[z])
            rows.append(slope_y + slope_z)
        result.append(jnp.stack(rows))
    return result


def first_kernel(line_ref, metric_ref, x_ref, ylo, yhi, zlo, zhi, out_ref, *operands):
    q = [line_ref[f] for f in range(5)]
    cross = slopes(q, ylo, yhi, zlo, zhi)
    scale = time_step * metric_ref[...]
    new = []
    for f in range(5):
        value = q[f] + scale * (x_ref[f] - cross[f])
        out_ref[f] = value
        new.append(value)
    emit_operands(new, *operands)


def first_section(line, metric, x, halos):
    return pl.pallas_call(
        first_kernel,
        grid=(8,),
        out_shape=[jax.ShapeDtypeStruct((5, ZB, YB, 1024), f32), *operand_shapes],
        in_specs=[line_spec, cell_spec, line_spec, yedge_spec, yedge_spec, zedge_spec, zedge_spec],
        out_specs=[line_spec, *operand_specs],
        compiler_params=params(),
        cost_estimate=cost(20000000, 16000000),
        name="first",
    )(line, metric, x, *halos)


def final_kernel(line_ref, first_ref, metric_ref, x_ref, ylo, yhi, zlo, zhi, out_ref, load_ref):
    q = [first_ref[f] for f in range(5)]
    cross = slopes(q, ylo, yhi, zlo, zhi)
    metric = metric_ref[...]
    scale = time_step * metric
    lane = lax.broadcasted_iota(jnp.int32, (8, YB, LANES), 2)
    final = []
    for f in range(5):
        value = 0.5 * line_ref[f] + 0.5 * (q[f] + scale * (x_ref[f] - cross[f]))
        final.append(value)
        low, high = value[0:8], value[8:16]
        out_ref[0, f * 8 : f * 8 + 8] = jnp.where(lane < HALF, low, pltpu.roll(high, HALF, 2))
        out_ref[1, f * 8 : f * 8 + 8] = jnp.where(lane < HALF, pltpu.roll(low, HALF, 2), high)
    pressure = pressure_of(final, 1.0 / final[0])
    load_ref[...] = (pressure - pressure_ref) * metric


def final_section(line, first, metric, x, halos):
    return pl.pallas_call(
        final_kernel,
        grid=(8,),
        out_shape=[
            jax.ShapeDtypeStruct((16, 40, YB, LANES), f32),
            jax.ShapeDtypeStruct((ZB, YB, 1024), f32),
        ],
        in_specs=[
            line_spec,
            line_spec,
            cell_spec,
            line_spec,
            yedge_spec,
            yedge_spec,
            zedge_spec,
            zedge_spec,
        ],
        out_specs=[pl.BlockSpec((2, 40, YB, LANES), lambda s: (s, 0, 0, 0)), cell_spec],
        compiler_params=params(),
        cost_estimate=cost(20000000, 14000000),
        name="final",
    )(line, first, metric, x, *halos)


def home_kernel(in_ref, d_ref, m_ref, e_ref):
    for zp in range(8):
        for f in range(5):
            tile = in_ref[:, f * 8 + zp].reshape(LANES, LANES).T
            if f == 0:
                dst = d_ref
            elif f < 4:
                dst = m_ref.at[f - 1]
            else:
                dst = e_ref
            dst[pl.ds(zp, XB, stride=ZB), :] = tile[0:HALF]
            dst[pl.ds(zp + 8, XB, stride=ZB), :] = tile[HALF:LANES]


def home(packed):
    vm = pl.BlockSpec(memory_space=pltpu.VMEM)
    d, m, e = pl.pallas_call(
        home_kernel,
        out_shape=[
            jax.ShapeDtypeStruct((XB * ZB, LANES), f32),
            jax.ShapeDtypeStruct((3, XB * ZB, LANES), f32),
            jax.ShapeDtypeStruct((XB * ZB, LANES), f32),
        ],
        in_specs=[vm],
        out_specs=[vm] * 3,
        compiler_params=params(),
        cost_estimate=cost(1000000, 5300000),
        name="home",
    )(packed)
    return (
        d.reshape(XB, ZB, LANES),
        m.reshape(3, XB, ZB, LANES),
        e.reshape(XB, ZB, LANES),
    )


def forces_kernel(load_ref, code_ref, table_ref, out_ref, sum_ref):
    sum_ref[...] = jnp.zeros_like(sum_ref)
    panel_row = lax.broadcasted_iota(jnp.int32, (NP, 1024), 0)
    shape_row = lax.broadcasted_iota(jnp.int32, (NSHAPE, 1024), 0)

    def step(z, carry):
        load = load_ref[z, pl.ds(0, 1), :]
        code = code_ref[pl.ds(z, 1), :].astype(jnp.int32)
        panel = code >> 8
        shape = code & 255
        high = load.astype(bf16)
        rest = load - high.astype(f32)
        middle = rest.astype(bf16)
        low = (rest - middle.astype(f32)).astype(bf16)
        hits = panel_row == panel
        pieces = [jnp.where(hits, piece.astype(f32), 0.0).astype(bf16) for piece in (high, middle, low)]
        shape_hits = jnp.where(shape_row == shape, 1.0, 0.0).astype(bf16)
        sum_ref[...] += lax.dot_general(
            jnp.concatenate(pieces, axis=0),
            shape_hits,
            (((1,), (1,)), ((), ())),
            preferred_element_type=f32,
        )
        return carry

    lax.fori_loop(0, ZB, step, 0)
    summed = sum_ref[0:NP] + sum_ref[NP : 2 * NP] + sum_ref[2 * NP : 3 * NP]
    out_ref[...] = jnp.dot(
        summed, table_ref[...], precision=lax.Precision.HIGHEST, preferred_element_type=f32
    )


def forces(load, code, table):
    vm = pl.BlockSpec(memory_space=pltpu.VMEM)
    return pl.pallas_call(
        forces_kernel,
        out_shape=jax.ShapeDtypeStruct((NP, LANES), f32),
        in_specs=[vm] * 3,
        out_specs=vm,
        scratch_shapes=[pltpu.VMEM((3 * NP, NSHAPE), f32)],
        compiler_params=params(),
        cost_estimate=cost(2 * 192 * 256 * 16384, 700000),
        name="forces",
    )(load, code, table)


def spread_forces(partial):
    me = lax.axis_index("gx")
    held = partial
    bit = 8
    while bit:
        half = held.shape[0] // 2
        pairs = [(g, g + bit) for g in range(0, 16, 2 * bit)]
        got = lax.ppermute(held[half:], "gx", pairs)
        held = jnp.where((me & bit) != 0, got, held[:half])
        bit //= 2
    for bit in (1, 2, 4):
        held = held + lax.ppermute(held, "gz", [(g, g ^ bit) for g in range(8)])
    return held


def exchange(ytop, ybot, ztop, zbot):
    up = [(g, g + 1) for g in range(15)]
    down = [(g + 1, g) for g in range(15)]
    right = [(g, (g + 1) % 8) for g in range(8)]
    left = [((g + 1) % 8, g) for g in range(8)]
    return (
        lax.ppermute(ytop, "gx", up),
        lax.ppermute(ybot, "gx", down),
        lax.ppermute(ztop, "gz", right),
        lax.ppermute(zbot, "gz", left),
    )


def split(matrix):
    high = lax.reduce_precision(matrix, 8, 7)
    return high.astype(bf16), (matrix - high).astype(bf16)


def body(
    density,
    momentum,
    energy,
    metric,
    deriv_matrix,
    smooth_matrix,
    panel_of_cell,
    shape_index,
    mode_table,
):
    outgoing = pack(density, momentum, energy, metric, panel_of_cell, shape_index)
    packed = lax.all_to_all(outgoing, "gx", split_axis=0, concat_axis=0, tiled=True)
    dhi, dlo = split(deriv_matrix.T)
    smooth = smooth_matrix.T.astype(bf16)
    sums = jnp.sum(smooth_matrix, axis=1).reshape(1, -1)
    packed, dhi, dlo, smooth, sums = lax.optimization_barrier((packed, dhi, dlo, smooth, sums))

    line, cells, code, q, fhi, flo, *edges = unpack(packed)
    halos = exchange(*edges)
    x = lines(q, fhi, flo, smooth, dhi, dlo, sums)
    first, q, fhi, flo, *edges = first_section(line, cells, x, halos)
    halos = exchange(*edges)
    x = lines(q, fhi, flo, smooth, dhi, dlo, sums)
    returning, load = final_section(line, first, cells, x, halos)

    packed = lax.all_to_all(returning, "gx", split_axis=0, concat_axis=0, tiled=True)
    panel_forces = spread_forces(forces(load, code, mode_table))
    new_density, new_momentum, new_energy = home(packed)
    return new_density, new_momentum, new_energy, panel_forces


def solution(mesh):
    in_specs = (
        P("gx", "gz", None),
        P(None, "gx", "gz", None),
        P("gx", "gz", None),
        P("gx", "gz", None),
        P(),
        P(),
        P("gx", "gz"),
        P("gx", "gz"),
        P(),
    )
    out_specs = (P("gx", "gz", None), P(None, "gx", "gz", None), P("gx", "gz", None), P("gx", None))
    return jax.shard_map(body, mesh=mesh, in_specs=in_specs, out_specs=out_specs, check_vma=False)
```

```python
import functools

import jax
import jax.numpy as jnp
from jax import lax
from jax.experimental import pallas as pl
from jax.experimental.pallas import tpu as pltpu
from jax.sharding import PartitionSpec as P

NP = 64
NSHAPE = 256
XB = 64
ZB = 16
YB = 8
LANES = 128
HALF = 64

time_step = 0.05
gas_factor = 0.4
pressure_ref = 2.0
middle = (1.5, 0.0, 0.0, 0.0, 5.0)
near = 8.0 / 12.0
far = 1.0 / 12.0

f32 = jnp.float32
bf16 = jnp.bfloat16


def grant(mib):
    return pltpu.CompilerParams(vmem_limit_bytes=mib * 1024 * 1024)


def cost(flops, nbytes):
    return pl.CostEstimate(flops=flops, bytes_accessed=nbytes, transcendentals=0)


def shaped(*shape):
    return jax.ShapeDtypeStruct(shape, f32)


def pressure_of(q, inverse):
    return gas_factor * (q[4] - 0.5 * (q[1] * q[1] + q[2] * q[2] + q[3] * q[3]) * inverse)


def flux(q, pressure, inverse, direction):
    speed = q[1 + direction] * inverse
    parts = [q[1 + direction]]
    for component in range(3):
        term = q[1 + component] * speed
        if component == direction:
            term = term + pressure
        parts.append(term)
    parts.append((q[4] + pressure) * speed)
    return parts


def turn(v, shift):
    shift = shift % YB
    return pltpu.roll(v, shift, v.ndim - 2) if shift else v


def pack_kernel(d_hbm, m_hbm, e_hbm, g_hbm, panel_ref, shape_ref, out_hbm, raw, tiles, code_ref, in_sem, out_sem):
    sources = [d_hbm, m_hbm.at[0], m_hbm.at[1], m_hbm.at[2], e_hbm, g_hbm]
    loads = [pltpu.make_async_copy(sources[f], raw.at[f], in_sem.at[f]) for f in range(6)]
    for load in loads:
        load.start()
    turned = (panel_ref[...] * NSHAPE + shape_ref[...]).astype(f32)
    for peer in range(16):
        code_ref[peer, :, 0:HALF] = turned[0:8]
        code_ref[peer, :, HALF:LANES] = turned[8:16]
    stores = [pltpu.make_async_copy(code_ref, out_hbm.at[:, 48], out_sem.at[6])]
    stores[0].start()
    for f in range(6):
        loads[f].wait()
        for zp in range(8):
            low = raw[f, pl.ds(zp, XB, stride=ZB), :]
            high = raw[f, pl.ds(zp + 8, XB, stride=ZB), :]
            tile = jnp.concatenate([low, high], axis=0).T
            tiles[f, :, zp] = tile.reshape(16, YB, LANES)
        store = pltpu.make_async_copy(tiles.at[f], out_hbm.at[:, f * 8 : f * 8 + 8], out_sem.at[f])
        store.start()
        stores.append(store)
    for store in stores:
        store.wait()


def pack(density, momentum, energy, metric, panels, shapes):
    vm = pl.BlockSpec(memory_space=pltpu.VMEM)
    hbm = pl.BlockSpec(memory_space=pl.ANY)
    return pl.pallas_call(
        pack_kernel,
        out_shape=shaped(16, 49, YB, LANES),
        in_specs=[hbm] * 4 + [vm] * 2,
        out_specs=hbm,
        scratch_shapes=[
            pltpu.VMEM((6, XB * ZB, LANES), f32),
            pltpu.VMEM((6, 16, 8, YB, LANES), f32),
            pltpu.VMEM((16, YB, LANES), f32),
            pltpu.SemaphoreType.DMA((6,)),
            pltpu.SemaphoreType.DMA((7,)),
        ],
        compiler_params=pltpu.CompilerParams(),
        cost_estimate=cost(1000000, 6400000),
        name="pack",
    )(
        density.reshape(XB * ZB, LANES),
        momentum.reshape(3, XB * ZB, LANES),
        energy.reshape(XB * ZB, LANES),
        metric.reshape(XB * ZB, LANES),
        panels.T,
        shapes.T,
    )


def emit_edges(q, inverse, pressure, up_ref, down_ref, right_ref, left_ref):
    row = lax.broadcasted_iota(jnp.int32, (YB, LANES), 0)
    even = row % 2 == 0
    normal = flux(q, pressure, inverse, 1)
    for f in range(5):
        for zq in range(4):
            top = bottom = None
            for z4 in range(4):
                plane = normal[f][zq * 4 + z4]
                last = turn(plane, 2 * z4 + 2)
                head = turn(plane, 2 * z4)
                mine = (row >= 2 * z4) & (row < 2 * z4 + 2)
                top = last if top is None else jnp.where(mine, last, top)
                bottom = head if bottom is None else jnp.where(mine, head, bottom)
            up_ref[f, zq] = far * top - jnp.where(even, near * turn(top, -1), 0.0)
            bottom = jnp.where(even, 0.0, near * turn(bottom, 1)) - far * bottom
            down_ref[f, zq] = turn(bottom, 6)
    ends = [q[f][0:2] for f in range(5)], [q[f][14:16] for f in range(5)]
    low = flux(ends[0], pressure[0:2], inverse[0:2], 2)
    high = flux(ends[1], pressure[14:16], inverse[14:16], 2)
    for f in range(5):
        left_ref[f, 0] = -far * low[f][0]
        left_ref[f, 1] = near * low[f][0] - far * low[f][1]
        right_ref[f, 0] = far * high[f][0] - near * high[f][1]
        right_ref[f, 1] = far * high[f][1]


edge_shapes = [shaped(5, 4, YB, 1024)] * 2 + [shaped(5, 2, YB, 1024)] * 2
yedge_spec = pl.BlockSpec((5, 4, YB, LANES), lambda s: (0, 0, 0, s))
zedge_spec = pl.BlockSpec((5, 2, YB, LANES), lambda s: (0, 0, 0, s))
edge_specs = [yedge_spec] * 2 + [zedge_spec] * 2
line_spec = pl.BlockSpec((5, ZB, YB, LANES), lambda s: (0, 0, 0, s))
cell_spec = pl.BlockSpec((ZB, YB, LANES), lambda s: (0, 0, s))
code_spec = pl.BlockSpec((ZB, LANES), lambda s: (0, s))


def missing(f, z, up_ref, down_ref, right_ref, left_ref):
    row = lax.broadcasted_iota(jnp.int32, (YB, LANES), 0)
    zq, z4 = z // 4, z % 4
    mine = (row >= 2 * z4) & (row < 2 * z4 + 2)
    both = turn(jnp.where(mine, up_ref[f, zq], down_ref[f, zq]), -2 * z4)
    value = jnp.where((row < 2) | (row > 5), both, 0.0)
    if z < 2:
        value = value + right_ref[f, z]
    if z > 13:
        value = value + left_ref[f, z - 14]
    return value


def exchange(up, down, right, left):
    ahead = [(g, g + 1) for g in range(15)]
    back = [(g + 1, g) for g in range(15)]
    return (
        lax.ppermute(up, "gx", ahead),
        lax.ppermute(down, "gx", back),
        lax.ppermute(right, "gz", [(g, (g + 1) % 8) for g in range(8)]),
        lax.ppermute(left, "gz", [((g + 1) % 8, g) for g in range(8)]),
    )


def join(a, b):
    lane = lax.broadcasted_iota(jnp.int32, a.shape, a.ndim - 1)
    axis = a.ndim - 1
    low = jnp.where(lane < HALF, a, pltpu.roll(b, HALF, axis))
    high = jnp.where(lane < HALF, pltpu.roll(a, HALF, axis), b)
    return jnp.concatenate([low, high], axis=0)


def unpack_kernel(in_ref, line_ref, metric_ref, code_ref, *edges):
    q = []
    for f in range(5):
        field = join(in_ref[0, f * 8 : f * 8 + 8], in_ref[1, f * 8 : f * 8 + 8])
        line_ref[f] = field
        q.append(field)
    metric_ref[...] = join(in_ref[0, 40:48], in_ref[1, 40:48])
    code_ref[...] = join(in_ref[0, 48], in_ref[1, 48])
    inverse = 1.0 / q[0]
    emit_edges(q, inverse, pressure_of(q, inverse), *edges)


def unpack(packed):
    return pl.pallas_call(
        unpack_kernel,
        grid=(8,),
        out_shape=[shaped(5, ZB, YB, 1024), shaped(ZB, YB, 1024), shaped(ZB, 1024), *edge_shapes],
        in_specs=[pl.BlockSpec((2, 49, YB, LANES), lambda s: (s, 0, 0, 0))],
        out_specs=[line_spec, cell_spec, code_spec, *edge_specs],
        compiler_params=grant(16),
        cost_estimate=cost(10000000, 8000000),
        name="unpack",
    )(packed)


def inner_slopes(q, f, normal, span):
    row = lax.broadcasted_iota(jnp.int32, (YB, LANES), 0)
    rows = []
    for z in range(ZB):
        g = normal[f][z]
        back1 = jnp.where(row < 1, 0.0, turn(g, 1))
        back2 = jnp.where(row < 2, 0.0, turn(g, 2))
        ahead1 = jnp.where(row > 6, 0.0, turn(g, -1))
        ahead2 = jnp.where(row > 5, 0.0, turn(g, -2))
        slope = near * (ahead1 - back1) - far * (ahead2 - back2)
        for offset, weight in ((1, near), (-1, -near), (2, -far), (-2, far)):
            if 0 <= z + offset < ZB:
                slope = slope + weight * span[f][z + offset]
        rows.append(slope)
    return jnp.stack(rows)


WIDE = 256


def inner_kernel(second, *refs):
    if second:
        whole_ref, base_ref, metric_ref, d_ref, s_ref, out_ref, q_ref, fhi_ref, flo_ref = refs
    else:
        whole_ref, metric_ref, d_ref, s_ref, out_ref, q_ref, fhi_ref, flo_ref = refs
    step = pl.program_id(0)

    @pl.when(step == 0)
    def prepare():
        def part(s, carry):
            lanes = pl.ds(pl.multiple_of(s * LANES, LANES), LANES)
            q = [whole_ref[f, :, :, lanes] for f in range(5)]
            inverse = 1.0 / q[0]
            stream = flux(q, pressure_of(q, inverse), inverse, 0)
            for f in range(5):
                rows = pl.ds(f * 128, 128)
                q_ref[rows, lanes] = (q[f] - middle[f]).reshape(128, LANES).astype(bf16)
                value = stream[f].reshape(128, LANES)
                high = value.astype(bf16)
                fhi_ref[rows, lanes] = high
                flo_ref[rows, lanes] = (value - high.astype(f32)).astype(bf16)
            return carry

        lax.fori_loop(0, 8, part, 0)

    dot = functools.partial(
        lax.dot_general,
        dimension_numbers=(((1,), (1,)), ((), ())),
        preferred_element_type=f32,
    )
    deriv = d_ref[...]
    dhi = deriv.astype(bf16)
    dlo = (deriv - dhi.astype(f32)).astype(bf16)
    smooth = s_ref[...]
    shi = smooth.astype(bf16)
    slo = (smooth - shi.astype(f32)).astype(bf16)
    ones = jnp.ones((16, 1024), bf16)
    sums = (dot(ones, shi) + dot(ones, slo))[0:1]
    fhi = fhi_ref[...]
    stream = dot(q_ref[...], shi) - (dot(fhi, dhi) + dot(flo_ref[...], dhi) + dot(fhi, dlo))
    for f in range(5):
        part = stream[f * 128 : f * 128 + 128]
        part = part + middle[f] * sums if middle[f] else part
        out_ref[f] = part.reshape(ZB, YB, WIDE)

    def finish(c, carry):
        near_lanes = pl.ds(pl.multiple_of(c * LANES, LANES), LANES)
        lanes = pl.ds(pl.multiple_of(step * WIDE + c * LANES, LANES), LANES)
        q = [whole_ref[f, :, :, lanes] for f in range(5)]
        inverse = 1.0 / q[0]
        pressure = pressure_of(q, inverse)
        normal = flux(q, pressure, inverse, 1)
        span = flux(q, pressure, inverse, 2)
        scale = time_step * metric_ref[:, :, near_lanes]
        for f in range(5):
            total = out_ref[f, :, :, near_lanes] - inner_slopes(q, f, normal, span)
            value = q[f] + scale * total
            if second:
                value = 0.5 * base_ref[f, :, :, near_lanes] + 0.5 * value
            out_ref[f, :, :, near_lanes] = value
        return carry

    lax.fori_loop(0, WIDE // LANES, finish, 0)


def inner(state, metric, deriv, smooth, base=None):
    second = base is not None
    whole = pl.BlockSpec((5, ZB, YB, 1024), lambda n: (0, 0, 0, 0))
    part = pl.BlockSpec((5, ZB, YB, WIDE), lambda n: (0, 0, 0, n))
    cell = pl.BlockSpec((ZB, YB, WIDE), lambda n: (0, 0, n))
    matrix = pl.BlockSpec((WIDE, 1024), lambda n: (n, 0))
    return pl.pallas_call(
        functools.partial(inner_kernel, second),
        grid=(1024 // WIDE,),
        out_shape=shaped(5, ZB, YB, 1024),
        in_specs=[whole] + ([part] if second else []) + [cell, matrix, matrix],
        out_specs=part,
        scratch_shapes=[pltpu.VMEM((640, 1024), bf16)] * 3,
        compiler_params=grant(26),
        cost_estimate=cost(8 * 640 * 1024 * 1024, 14000000),
        name="inner2" if second else "inner1",
    )(state, *([base] if second else []), metric, deriv, smooth)


def first_kernel(part_ref, metric_ref, up, down, right, left, out_ref, *edges):
    scale = time_step * metric_ref[...]
    new = []
    for f in range(5):
        halo = jnp.stack([missing(f, z, up, down, right, left) for z in range(ZB)])
        value = part_ref[f] - scale * halo
        out_ref[f] = value
        new.append(value)
    inverse = 1.0 / new[0]
    emit_edges(new, inverse, pressure_of(new, inverse), *edges)


def first_section(part, metric, halos):
    return pl.pallas_call(
        first_kernel,
        grid=(8,),
        out_shape=[shaped(5, ZB, YB, 1024), *edge_shapes],
        in_specs=[line_spec, cell_spec, *edge_specs],
        out_specs=[line_spec, *edge_specs],
        compiler_params=grant(16),
        cost_estimate=cost(10000000, 9000000),
        name="first",
    )(part, metric, *halos)


def final_kernel(part_ref, metric_ref, up, down, right, left, out_ref, load_ref):
    metric = metric_ref[...]
    scale = (0.5 * time_step) * metric
    lane = lax.broadcasted_iota(jnp.int32, (8, YB, LANES), 2)
    final = []
    for f in range(5):
        halo = jnp.stack([missing(f, z, up, down, right, left) for z in range(ZB)])
        value = part_ref[f] - scale * halo
        final.append(value)
        low, high = value[0:8], value[8:16]
        out_ref[0, f * 8 : f * 8 + 8] = jnp.where(lane < HALF, low, pltpu.roll(high, HALF, 2))
        out_ref[1, f * 8 : f * 8 + 8] = jnp.where(lane < HALF, pltpu.roll(low, HALF, 2), high)
    load_ref[...] = (pressure_of(final, 1.0 / final[0]) - pressure_ref) * metric


def final_section(part, metric, halos):
    return pl.pallas_call(
        final_kernel,
        grid=(8,),
        out_shape=[pltpu.HBM((16, 40, YB, LANES), f32), shaped(ZB, YB, 1024)],
        in_specs=[line_spec, cell_spec, *edge_specs],
        out_specs=[pl.BlockSpec((2, 40, YB, LANES), lambda s: (s, 0, 0, 0)), cell_spec],
        compiler_params=grant(16),
        cost_estimate=cost(10000000, 9000000),
        name="final",
    )(part, metric, *halos)


def home_kernel(in_ref, d_hbm, m_hbm, e_hbm, flat, sem):
    targets = [d_hbm, m_hbm.at[0], m_hbm.at[1], m_hbm.at[2], e_hbm]
    stores = []
    for f in range(5):
        for zp in range(8):
            tile = in_ref[:, f * 8 + zp].reshape(LANES, LANES).T
            flat[f, pl.ds(zp, XB, stride=ZB), :] = tile[0:HALF]
            flat[f, pl.ds(zp + 8, XB, stride=ZB), :] = tile[HALF:LANES]
        store = pltpu.make_async_copy(flat.at[f], targets[f], sem.at[f])
        store.start()
        stores.append(store)
    for store in stores:
        store.wait()


def home(packed):
    vm = pl.BlockSpec(memory_space=pltpu.VMEM)
    hbm = pl.BlockSpec(memory_space=pl.ANY)
    d, m, e = pl.pallas_call(
        home_kernel,
        out_shape=[shaped(XB * ZB, LANES), shaped(3, XB * ZB, LANES), shaped(XB * ZB, LANES)],
        in_specs=[vm],
        out_specs=[hbm] * 3,
        scratch_shapes=[pltpu.VMEM((5, XB * ZB, LANES), f32), pltpu.SemaphoreType.DMA((5,))],
        compiler_params=grant(16),
        cost_estimate=cost(1000000, 5300000),
        name="home",
    )(packed)
    return (
        d.reshape(XB, ZB, LANES),
        m.reshape(3, XB, ZB, LANES),
        e.reshape(XB, ZB, LANES),
    )


def forces_kernel(load_ref, code_ref, table_ref, out_ref, sum_ref):
    sum_ref[...] = jnp.zeros_like(sum_ref)
    run_row = lax.broadcasted_iota(jnp.int32, (8, 1024), 0)
    shape_row = lax.broadcasted_iota(jnp.int32, (NSHAPE, 1024), 0).astype(f32).astype(bf16)
    one = jnp.ones((NSHAPE, 1024), bf16)
    none = jnp.zeros((NSHAPE, 1024), bf16)

    def step(z, carry):
        load = load_ref[z, pl.ds(0, 1), :]
        code = code_ref[pl.ds(z, 1), :].astype(jnp.int32)
        across = code[:, 0:1] >> 11
        along = (code >> 8) & 7
        shape = (code & 255).astype(f32).astype(bf16)
        hit = jnp.where(run_row == along, load, 0.0)
        high = hit.astype(bf16)
        low = (hit - high.astype(f32)).astype(bf16)
        shape_hits = jnp.where(shape_row == shape, one, none)
        both = lax.dot_general(
            jnp.concatenate([high, low], axis=0),
            shape_hits,
            (((1,), (1,)), ((), ())),
            preferred_element_type=f32,
        )
        both = both[0:8] + both[8:16]
        for r in range(8):
            sum_ref[r * 8 : r * 8 + 8] += jnp.where(across == r, both, 0.0)
        return carry

    lax.fori_loop(0, ZB, step, 0)
    out_ref[...] = jnp.dot(
        sum_ref[...], table_ref[...], precision=lax.Precision.HIGHEST, preferred_element_type=f32
    )


def forces(load, code, table):
    vm = pl.BlockSpec(memory_space=pltpu.VMEM)
    return pl.pallas_call(
        forces_kernel,
        out_shape=shaped(NP, LANES),
        in_specs=[vm] * 3,
        out_specs=vm,
        scratch_shapes=[pltpu.VMEM((NP, NSHAPE), f32)],
        compiler_params=grant(16),
        cost_estimate=cost(2 * 16 * 256 * 16384, 700000),
        name="forces",
    )(load, code, table)


def spread_forces(held):
    for bit in (1, 2, 4):
        held = held + lax.ppermute(held, "gz", [(g, g ^ bit) for g in range(8)])
    me = lax.axis_index("gx")
    bit = 8
    while bit:
        half = held.shape[0] // 2
        got = lax.ppermute(held[half:], "gx", [(g, g + bit) for g in range(0, 16, 2 * bit)])
        held = jnp.where((me & bit) != 0, got, held[:half])
        bit //= 2
    return held


def body(
    density,
    momentum,
    energy,
    metric,
    deriv_matrix,
    smooth_matrix,
    panel_of_cell,
    shape_index,
    mode_table,
):
    outgoing = pack(density, momentum, energy, metric, panel_of_cell, shape_index)
    packed = lax.all_to_all(outgoing, "gx", split_axis=0, concat_axis=0, tiled=True)
    state, cells, code, *edges = unpack(packed)
    halos = exchange(*edges)
    part = inner(state, cells, deriv_matrix, smooth_matrix)
    first, *edges = first_section(part, cells, halos)
    halos = exchange(*edges)
    part = inner(first, cells, deriv_matrix, smooth_matrix, base=state)
    returning, load = final_section(part, cells, halos)
    packed = lax.all_to_all(returning, "gx", split_axis=0, concat_axis=0, tiled=True)
    panel_forces = spread_forces(forces(load, code, mode_table))
    new_density, new_momentum, new_energy = home(packed)
    return new_density, new_momentum, new_energy, panel_forces


def solution(mesh):
    in_specs = (
        P("gx", "gz", None),
        P(None, "gx", "gz", None),
        P("gx", "gz", None),
        P("gx", "gz", None),
        P(),
        P(),
        P("gx", "gz"),
        P("gx", "gz"),
        P(),
    )
    out_specs = (P("gx", "gz", None), P(None, "gx", "gz", None), P("gx", "gz", None), P("gx", None))
    return jax.shard_map(body, mesh=mesh, in_specs=in_specs, out_specs=out_specs, check_vma=False)
```

```python
import functools

import jax
import jax.numpy as jnp
from jax import lax
from jax.experimental import pallas as pl
from jax.experimental.pallas import tpu as pltpu
from jax.sharding import PartitionSpec as P

NP = 64
NSHAPE = 256
XB = 64
ZB = 16
YB = 8
LANES = 128
HALF = 64

time_step = 0.05
gas_factor = 0.4
pressure_ref = 2.0
middle = (1.5, 0.0, 0.0, 0.0, 5.0)
near = 8.0 / 12.0
far = 1.0 / 12.0

SNAKE = tuple(g if (g // 4) % 2 == 0 else 4 * (g // 4) + 3 - g % 4 for g in range(16))

f32 = jnp.float32
bf16 = jnp.bfloat16


def grant(mib):
    return pltpu.CompilerParams(vmem_limit_bytes=mib * 1024 * 1024)


def cost(flops, nbytes):
    return pl.CostEstimate(flops=flops, bytes_accessed=nbytes, transcendentals=0)


def shaped(*shape):
    return jax.ShapeDtypeStruct(shape, f32)


def pressure_of(q, inverse):
    return gas_factor * (q[4] - 0.5 * (q[1] * q[1] + q[2] * q[2] + q[3] * q[3]) * inverse)


def flux(q, pressure, inverse, direction):
    speed = q[1 + direction] * inverse
    parts = [q[1 + direction]]
    for component in range(3):
        term = q[1 + component] * speed
        if component == direction:
            term = term + pressure
        parts.append(term)
    parts.append((q[4] + pressure) * speed)
    return parts


def turn(v, shift):
    shift = shift % YB
    return pltpu.roll(v, shift, v.ndim - 2) if shift else v


def pack_kernel(d_hbm, m_hbm, e_hbm, g_hbm, panel_ref, shape_ref, out_hbm, raw, tiles, code_ref, in_sem, out_sem):
    sources = [d_hbm, m_hbm.at[0], m_hbm.at[1], m_hbm.at[2], e_hbm, g_hbm]
    loads = [pltpu.make_async_copy(sources[f], raw.at[f], in_sem.at[f]) for f in range(6)]
    for load in loads:
        load.start()
    turned = (panel_ref[...] * NSHAPE + shape_ref[...]).astype(f32)
    for peer in range(16):
        code_ref[peer, :, 0:HALF] = turned[0:8]
        code_ref[peer, :, HALF:LANES] = turned[8:16]
    stores = [pltpu.make_async_copy(code_ref, out_hbm.at[:, 48], out_sem.at[6])]
    stores[0].start()
    for f in range(6):
        loads[f].wait()
        for zp in range(8):
            low = raw[f, pl.ds(zp, XB, stride=ZB), :]
            high = raw[f, pl.ds(zp + 8, XB, stride=ZB), :]
            tile = jnp.concatenate([low, high], axis=0).T
            for peer in range(16):
                tiles[f, peer, zp] = tile[SNAKE[peer] * YB : SNAKE[peer] * YB + YB]
        store = pltpu.make_async_copy(tiles.at[f], out_hbm.at[:, f * 8 : f * 8 + 8], out_sem.at[f])
        store.start()
        stores.append(store)
    for store in stores:
        store.wait()


def pack(density, momentum, energy, metric, panels, shapes):
    vm = pl.BlockSpec(memory_space=pltpu.VMEM)
    hbm = pl.BlockSpec(memory_space=pl.ANY)
    return pl.pallas_call(
        pack_kernel,
        out_shape=shaped(16, 49, YB, LANES),
        in_specs=[hbm] * 4 + [vm] * 2,
        out_specs=hbm,
        scratch_shapes=[
            pltpu.VMEM((6, XB * ZB, LANES), f32),
            pltpu.VMEM((6, 16, 8, YB, LANES), f32),
            pltpu.VMEM((16, YB, LANES), f32),
            pltpu.SemaphoreType.DMA((6,)),
            pltpu.SemaphoreType.DMA((7,)),
        ],
        compiler_params=pltpu.CompilerParams(),
        cost_estimate=cost(1000000, 6400000),
        name="pack",
    )(
        density.reshape(XB * ZB, LANES),
        momentum.reshape(3, XB * ZB, LANES),
        energy.reshape(XB * ZB, LANES),
        metric.reshape(XB * ZB, LANES),
        panels.T,
        shapes.T,
    )


def emit_edges(q, inverse, pressure, up_ref, down_ref, right_ref, left_ref):
    row = lax.broadcasted_iota(jnp.int32, (YB, LANES), 0)
    even = row % 2 == 0
    normal = flux(q, pressure, inverse, 1)
    for f in range(5):
        for zq in range(4):
            top = bottom = None
            for z4 in range(4):
                plane = normal[f][zq * 4 + z4]
                last = turn(plane, 2 * z4 + 2)
                head = turn(plane, 2 * z4)
                mine = (row >= 2 * z4) & (row < 2 * z4 + 2)
                top = last if top is None else jnp.where(mine, last, top)
                bottom = head if bottom is None else jnp.where(mine, head, bottom)
            up_ref[f, zq] = far * top - jnp.where(even, near * turn(top, -1), 0.0)
            bottom = jnp.where(even, 0.0, near * turn(bottom, 1)) - far * bottom
            down_ref[f, zq] = turn(bottom, 6)
    ends = [q[f][0:2] for f in range(5)], [q[f][14:16] for f in range(5)]
    low = flux(ends[0], pressure[0:2], inverse[0:2], 2)
    high = flux(ends[1], pressure[14:16], inverse[14:16], 2)
    for f in range(5):
        left_ref[f, 0] = -far * low[f][0]
        left_ref[f, 1] = near * low[f][0] - far * low[f][1]
        right_ref[f, 0] = far * high[f][0] - near * high[f][1]
        right_ref[f, 1] = far * high[f][1]


edge_shapes = [shaped(5, 4, YB, 1024)] * 2 + [shaped(5, 2, YB, 1024)] * 2
yedge_spec = pl.BlockSpec((5, 4, YB, LANES), lambda s: (0, 0, 0, s))
zedge_spec = pl.BlockSpec((5, 2, YB, LANES), lambda s: (0, 0, 0, s))
edge_specs = [yedge_spec] * 2 + [zedge_spec] * 2
line_spec = pl.BlockSpec((5, ZB, YB, LANES), lambda s: (0, 0, 0, s))
cell_spec = pl.BlockSpec((ZB, YB, LANES), lambda s: (0, 0, s))
code_spec = pl.BlockSpec((ZB, LANES), lambda s: (0, s))


def missing(f, z, up_ref, down_ref, right_ref, left_ref):
    row = lax.broadcasted_iota(jnp.int32, (YB, LANES), 0)
    zq, z4 = z // 4, z % 4
    mine = (row >= 2 * z4) & (row < 2 * z4 + 2)
    both = turn(jnp.where(mine, up_ref[f, zq], down_ref[f, zq]), -2 * z4)
    value = jnp.where((row < 2) | (row > 5), both, 0.0)
    if z < 2:
        value = value + right_ref[f, z]
    if z > 13:
        value = value + left_ref[f, z - 14]
    return value


def exchange(up, down, right, left):
    ahead = [(SNAKE[b], SNAKE[b + 1]) for b in range(15)]
    back = [(SNAKE[b + 1], SNAKE[b]) for b in range(15)]
    return (
        lax.ppermute(up, "gx", ahead),
        lax.ppermute(down, "gx", back),
        lax.ppermute(right, "gz", [(g, (g + 1) % 8) for g in range(8)]),
        lax.ppermute(left, "gz", [((g + 1) % 8, g) for g in range(8)]),
    )


def join(a, b):
    lane = lax.broadcasted_iota(jnp.int32, a.shape, a.ndim - 1)
    axis = a.ndim - 1
    low = jnp.where(lane < HALF, a, pltpu.roll(b, HALF, axis))
    high = jnp.where(lane < HALF, pltpu.roll(a, HALF, axis), b)
    return jnp.concatenate([low, high], axis=0)


def unpack_kernel(in_ref, line_ref, metric_ref, code_ref, *edges):
    q = []
    for f in range(5):
        field = join(in_ref[0, f * 8 : f * 8 + 8], in_ref[1, f * 8 : f * 8 + 8])
        line_ref[f] = field
        q.append(field)
    metric_ref[...] = join(in_ref[0, 40:48], in_ref[1, 40:48])
    code_ref[...] = join(in_ref[0, 48], in_ref[1, 48])
    inverse = 1.0 / q[0]
    emit_edges(q, inverse, pressure_of(q, inverse), *edges)


def unpack(packed):
    return pl.pallas_call(
        unpack_kernel,
        grid=(8,),
        out_shape=[shaped(5, ZB, YB, 1024), shaped(ZB, YB, 1024), shaped(ZB, 1024), *edge_shapes],
        in_specs=[pl.BlockSpec((2, 49, YB, LANES), lambda s: (s, 0, 0, 0))],
        out_specs=[line_spec, cell_spec, code_spec, *edge_specs],
        compiler_params=grant(16),
        cost_estimate=cost(10000000, 8000000),
        name="unpack",
    )(packed)


def inner_slopes(q, f, normal, span):
    row = lax.broadcasted_iota(jnp.int32, (YB, LANES), 0)
    rows = []
    for z in range(ZB):
        g = normal[f][z]
        back1 = jnp.where(row < 1, 0.0, turn(g, 1))
        back2 = jnp.where(row < 2, 0.0, turn(g, 2))
        ahead1 = jnp.where(row > 6, 0.0, turn(g, -1))
        ahead2 = jnp.where(row > 5, 0.0, turn(g, -2))
        slope = near * (ahead1 - back1) - far * (ahead2 - back2)
        for offset, weight in ((1, near), (-1, -near), (2, -far), (-2, far)):
            if 0 <= z + offset < ZB:
                slope = slope + weight * span[f][z + offset]
        rows.append(slope)
    return jnp.stack(rows)


WIDE = 256


def inner_kernel(second, *refs):
    if second:
        whole_ref, base_ref, metric_ref, d_ref, s_ref, out_ref, q_ref, fhi_ref, flo_ref, slope_ref = refs
    else:
        whole_ref, metric_ref, d_ref, s_ref, out_ref, q_ref, fhi_ref, flo_ref, slope_ref = refs
    step = pl.program_id(0)

    @pl.when(step == 0)
    def prepare():
        def part(s, carry):
            lanes = pl.ds(pl.multiple_of(s * LANES, LANES), LANES)
            q = [whole_ref[f, :, :, lanes] for f in range(5)]
            inverse = 1.0 / q[0]
            stream = flux(q, pressure_of(q, inverse), inverse, 0)
            for f in range(5):
                rows = pl.ds(f * 128, 128)
                q_ref[rows, lanes] = (q[f] - middle[f]).reshape(128, LANES).astype(bf16)
                value = stream[f].reshape(128, LANES)
                high = value.astype(bf16)
                fhi_ref[rows, lanes] = high
                flo_ref[rows, lanes] = (value - high.astype(f32)).astype(bf16)
            return carry

        lax.fori_loop(0, 8, part, 0)

    wide = pl.ds(pl.multiple_of(step * WIDE, WIDE), WIDE)
    for c in range(WIDE // LANES):
        lanes = pl.ds(pl.multiple_of(step * WIDE + c * LANES, LANES), LANES)
        q = [whole_ref[f, :, :, lanes] for f in range(5)]
        inverse = 1.0 / q[0]
        pressure = pressure_of(q, inverse)
        normal = flux(q, pressure, inverse, 1)
        span = flux(q, pressure, inverse, 2)
        for f in range(5):
            slope_ref[f, :, :, c * LANES : c * LANES + LANES] = inner_slopes(q, f, normal, span)

    dot = functools.partial(
        lax.dot_general,
        dimension_numbers=(((1,), (1,)), ((), ())),
        preferred_element_type=f32,
    )
    deriv = d_ref[...]
    dhi = deriv.astype(bf16)
    dlo = (deriv - dhi.astype(f32)).astype(bf16)
    smooth = s_ref[...]
    shi = smooth.astype(bf16)
    slo = (smooth - shi.astype(f32)).astype(bf16)
    ones = jnp.ones((16, 1024), bf16)
    sums = (dot(ones, shi) + dot(ones, slo))[0:1]
    fhi = fhi_ref[...]
    stream = dot(q_ref[...], shi) - (dot(fhi, dhi) + dot(flo_ref[...], dhi) + dot(fhi, dlo))
    for f in range(5):
        part = stream[f * 128 : f * 128 + 128]
        part = part + middle[f] * sums if middle[f] else part
        out_ref[f] = part.reshape(ZB, YB, WIDE)

    for f in range(5):
        value = whole_ref[f, :, :, wide] + time_step * metric_ref[...] * (out_ref[f] - slope_ref[f])
        if second:
            value = 0.5 * base_ref[f] + 0.5 * value
        out_ref[f] = value


def inner(state, metric, deriv, smooth, base=None):
    second = base is not None
    whole = pl.BlockSpec((5, ZB, YB, 1024), lambda n: (0, 0, 0, 0))
    part = pl.BlockSpec((5, ZB, YB, WIDE), lambda n: (0, 0, 0, n))
    cell = pl.BlockSpec((ZB, YB, WIDE), lambda n: (0, 0, n))
    matrix = pl.BlockSpec((WIDE, 1024), lambda n: (n, 0))
    return pl.pallas_call(
        functools.partial(inner_kernel, second),
        grid=(1024 // WIDE,),
        out_shape=shaped(5, ZB, YB, 1024),
        in_specs=[whole] + ([part] if second else []) + [cell, matrix, matrix],
        out_specs=part,
        scratch_shapes=[pltpu.VMEM((640, 1024), bf16)] * 3 + [pltpu.VMEM((5, ZB, YB, WIDE), f32)],
        compiler_params=grant(26),
        cost_estimate=cost(8 * 640 * 1024 * 1024, 14000000),
        name="inner2" if second else "inner1",
    )(state, *([base] if second else []), metric, deriv, smooth)


def first_kernel(part_ref, metric_ref, up, down, right, left, out_ref, *edges):
    scale = time_step * metric_ref[...]
    new = []
    for f in range(5):
        halo = jnp.stack([missing(f, z, up, down, right, left) for z in range(ZB)])
        value = part_ref[f] - scale * halo
        out_ref[f] = value
        new.append(value)
    inverse = 1.0 / new[0]
    emit_edges(new, inverse, pressure_of(new, inverse), *edges)


def first_section(part, metric, halos):
    return pl.pallas_call(
        first_kernel,
        grid=(8,),
        out_shape=[shaped(5, ZB, YB, 1024), *edge_shapes],
        in_specs=[line_spec, cell_spec, *edge_specs],
        out_specs=[line_spec, *edge_specs],
        compiler_params=grant(16),
        cost_estimate=cost(10000000, 9000000),
        name="first",
    )(part, metric, *halos)


def final_kernel(part_ref, metric_ref, up, down, right, left, out_ref, load_ref):
    metric = metric_ref[...]
    scale = (0.5 * time_step) * metric
    lane = lax.broadcasted_iota(jnp.int32, (8, YB, LANES), 2)
    final = []
    for f in range(5):
        halo = jnp.stack([missing(f, z, up, down, right, left) for z in range(ZB)])
        value = part_ref[f] - scale * halo
        final.append(value)
        low, high = value[0:8], value[8:16]
        out_ref[0, f * 8 : f * 8 + 8] = jnp.where(lane < HALF, low, pltpu.roll(high, HALF, 2))
        out_ref[1, f * 8 : f * 8 + 8] = jnp.where(lane < HALF, pltpu.roll(low, HALF, 2), high)
    load_ref[...] = (pressure_of(final, 1.0 / final[0]) - pressure_ref) * metric


def final_section(part, metric, halos):
    return pl.pallas_call(
        final_kernel,
        grid=(8,),
        out_shape=[pltpu.HBM((16, 40, YB, LANES), f32), shaped(ZB, YB, 1024)],
        in_specs=[line_spec, cell_spec, *edge_specs],
        out_specs=[pl.BlockSpec((2, 40, YB, LANES), lambda s: (s, 0, 0, 0)), cell_spec],
        compiler_params=grant(16),
        cost_estimate=cost(10000000, 9000000),
        name="final",
    )(part, metric, *halos)


def home_kernel(in_ref, d_hbm, m_hbm, e_hbm, flat, sem):
    targets = [d_hbm, m_hbm.at[0], m_hbm.at[1], m_hbm.at[2], e_hbm]
    stores = []
    for f in range(5):
        for zp in range(8):
            tile = jnp.concatenate([in_ref[SNAKE[b], f * 8 + zp] for b in range(16)], axis=0).T
            flat[f, pl.ds(zp, XB, stride=ZB), :] = tile[0:HALF]
            flat[f, pl.ds(zp + 8, XB, stride=ZB), :] = tile[HALF:LANES]
        store = pltpu.make_async_copy(flat.at[f], targets[f], sem.at[f])
        store.start()
        stores.append(store)
    for store in stores:
        store.wait()


def home(packed):
    vm = pl.BlockSpec(memory_space=pltpu.VMEM)
    hbm = pl.BlockSpec(memory_space=pl.ANY)
    d, m, e = pl.pallas_call(
        home_kernel,
        out_shape=[shaped(XB * ZB, LANES), shaped(3, XB * ZB, LANES), shaped(XB * ZB, LANES)],
        in_specs=[vm],
        out_specs=[hbm] * 3,
        scratch_shapes=[pltpu.VMEM((5, XB * ZB, LANES), f32), pltpu.SemaphoreType.DMA((5,))],
        compiler_params=grant(16),
        cost_estimate=cost(1000000, 5300000),
        name="home",
    )(packed)
    return (
        d.reshape(XB, ZB, LANES),
        m.reshape(3, XB, ZB, LANES),
        e.reshape(XB, ZB, LANES),
    )


def forces_kernel(load_ref, code_ref, table_ref, out_ref, sum_ref):
    sum_ref[...] = jnp.zeros_like(sum_ref)
    run_row = lax.broadcasted_iota(jnp.int32, (8, 1024), 0)
    shape_row = lax.broadcasted_iota(jnp.int32, (NSHAPE, 1024), 0).astype(f32).astype(bf16)
    one = jnp.ones((NSHAPE, 1024), bf16)
    none = jnp.zeros((NSHAPE, 1024), bf16)

    def step(z, carry):
        load = load_ref[z, pl.ds(0, 1), :]
        code = code_ref[pl.ds(z, 1), :].astype(jnp.int32)
        across = code[:, 0:1] >> 11
        along = (code >> 8) & 7
        shape = (code & 255).astype(f32).astype(bf16)
        hit = jnp.where(run_row == along, load, 0.0)
        high = hit.astype(bf16)
        low = (hit - high.astype(f32)).astype(bf16)
        shape_hits = jnp.where(shape_row == shape, one, none)
        both = lax.dot_general(
            jnp.concatenate([high, low], axis=0),
            shape_hits,
            (((1,), (1,)), ((), ())),
            preferred_element_type=f32,
        )
        both = both[0:8] + both[8:16]
        for r in range(8):
            sum_ref[r * 8 : r * 8 + 8] += jnp.where(across == r, both, 0.0)
        return carry

    lax.fori_loop(0, ZB, step, 0)
    out_ref[...] = jnp.dot(
        sum_ref[...], table_ref[...], precision=lax.Precision.HIGHEST, preferred_element_type=f32
    )


def forces(load, code, table):
    vm = pl.BlockSpec(memory_space=pltpu.VMEM)
    return pl.pallas_call(
        forces_kernel,
        out_shape=shaped(NP, LANES),
        in_specs=[vm] * 3,
        out_specs=vm,
        scratch_shapes=[pltpu.VMEM((NP, NSHAPE), f32)],
        compiler_params=grant(16),
        cost_estimate=cost(2 * 16 * 256 * 16384, 700000),
        name="forces",
    )(load, code, table)


def spread_forces(held):
    for bit in (1, 2, 4):
        held = held + lax.ppermute(held, "gz", [(g, g ^ bit) for g in range(8)])
    me = lax.axis_index("gx")
    bit = 8
    while bit:
        half = held.shape[0] // 2
        got = lax.ppermute(held[half:], "gx", [(g, g + bit) for g in range(0, 16, 2 * bit)])
        held = jnp.where((me & bit) != 0, got, held[:half])
        bit //= 2
    return held


def body(
    density,
    momentum,
    energy,
    metric,
    deriv_matrix,
    smooth_matrix,
    panel_of_cell,
    shape_index,
    mode_table,
):
    outgoing = pack(density, momentum, energy, metric, panel_of_cell, shape_index)
    packed = lax.all_to_all(outgoing, "gx", split_axis=0, concat_axis=0, tiled=True)
    state, cells, code, *edges = unpack(packed)
    halos = exchange(*edges)
    part = inner(state, cells, deriv_matrix, smooth_matrix)
    first, *edges = first_section(part, cells, halos)
    halos = exchange(*edges)
    part = inner(first, cells, deriv_matrix, smooth_matrix, base=state)
    returning, load = final_section(part, cells, halos)
    packed = lax.all_to_all(returning, "gx", split_axis=0, concat_axis=0, tiled=True)
    panel_forces = spread_forces(forces(load, code, mode_table))
    new_density, new_momentum, new_energy = home(packed)
    return new_density, new_momentum, new_energy, panel_forces


def solution(mesh):
    in_specs = (
        P("gx", "gz", None),
        P(None, "gx", "gz", None),
        P("gx", "gz", None),
        P("gx", "gz", None),
        P(),
        P(),
        P("gx", "gz"),
        P("gx", "gz"),
        P(),
    )
    out_specs = (P("gx", "gz", None), P(None, "gx", "gz", None), P("gx", "gz", None), P("gx", None))
    return jax.shard_map(body, mesh=mesh, in_specs=in_specs, out_specs=out_specs, check_vma=False)
```

```python
import functools

import jax
import jax.numpy as jnp
from jax import lax
from jax.experimental import pallas as pl
from jax.experimental.pallas import tpu as pltpu
from jax.sharding import PartitionSpec as P

NP = 64
NSHAPE = 256
XB = 64
ZB = 16
YB = 8
LANES = 128
HALF = 64

time_step = 0.05
gas_factor = 0.4
pressure_ref = 2.0
middle = (1.5, 0.0, 0.0, 0.0, 5.0)
near = 8.0 / 12.0
far = 1.0 / 12.0

SNAKE = tuple(g if (g // 4) % 2 == 0 else 4 * (g // 4) + 3 - g % 4 for g in range(16))

f32 = jnp.float32
bf16 = jnp.bfloat16


def grant(mib):
    return pltpu.CompilerParams(vmem_limit_bytes=mib * 1024 * 1024)


def cost(flops, nbytes):
    return pl.CostEstimate(flops=flops, bytes_accessed=nbytes, transcendentals=0)


def shaped(*shape):
    return jax.ShapeDtypeStruct(shape, f32)


def pressure_of(q, inverse):
    return gas_factor * (q[4] - 0.5 * (q[1] * q[1] + q[2] * q[2] + q[3] * q[3]) * inverse)


def flux(q, pressure, inverse, direction):
    speed = q[1 + direction] * inverse
    parts = [q[1 + direction]]
    for component in range(3):
        term = q[1 + component] * speed
        if component == direction:
            term = term + pressure
        parts.append(term)
    parts.append((q[4] + pressure) * speed)
    return parts


def turn(v, shift):
    shift = shift % YB
    return pltpu.roll(v, shift, v.ndim - 2) if shift else v


def pack_kernel(
    d_hbm, m_hbm, e_hbm, g_hbm, panel_hbm, shape_hbm, out_hbm, raw, tiles, index, code_ref, in_sem, out_sem
):
    sources = [d_hbm, m_hbm.at[0], m_hbm.at[1], m_hbm.at[2], e_hbm, g_hbm]
    loads = [pltpu.make_async_copy(sources[f], raw.at[f], in_sem.at[f]) for f in range(6)]
    loads += [
        pltpu.make_async_copy(panel_hbm, index.at[0], in_sem.at[6]),
        pltpu.make_async_copy(shape_hbm, index.at[1], in_sem.at[7]),
    ]
    for load in loads:
        load.start()
    stores = []
    for f in range(6):
        if f == 5:
            loads[6].wait()
            loads[7].wait()
            turned = (index[0] * NSHAPE + index[1]).astype(f32)
            for peer in range(16):
                code_ref[peer, :, 0:HALF] = turned[0:8]
                code_ref[peer, :, HALF:LANES] = turned[8:16]
            store = pltpu.make_async_copy(code_ref, out_hbm.at[:, 48], out_sem.at[6])
            store.start()
            stores.append(store)
        loads[f].wait()
        for zp in range(8):
            low = raw[f, pl.ds(zp, XB, stride=ZB), :]
            high = raw[f, pl.ds(zp + 8, XB, stride=ZB), :]
            tile = jnp.concatenate([low, high], axis=0).T
            for peer in range(16):
                tiles[f, peer, zp] = tile[SNAKE[peer] * YB : SNAKE[peer] * YB + YB]
        store = pltpu.make_async_copy(tiles.at[f], out_hbm.at[:, f * 8 : f * 8 + 8], out_sem.at[f])
        store.start()
        stores.append(store)
    for store in stores:
        store.wait()


def pack(density, momentum, energy, metric, panels, shapes):
    hbm = pl.BlockSpec(memory_space=pl.ANY)
    return pl.pallas_call(
        pack_kernel,
        out_shape=shaped(16, 49, YB, LANES),
        in_specs=[hbm] * 6,
        out_specs=hbm,
        scratch_shapes=[
            pltpu.VMEM((6, XB * ZB, LANES), f32),
            pltpu.VMEM((6, 16, 8, YB, LANES), f32),
            pltpu.VMEM((2, ZB, XB), jnp.int32),
            pltpu.VMEM((16, YB, LANES), f32),
            pltpu.SemaphoreType.DMA((8,)),
            pltpu.SemaphoreType.DMA((7,)),
        ],
        compiler_params=pltpu.CompilerParams(),
        cost_estimate=cost(1000000, 6400000),
        name="pack",
    )(
        density.reshape(XB * ZB, LANES),
        momentum.reshape(3, XB * ZB, LANES),
        energy.reshape(XB * ZB, LANES),
        metric.reshape(XB * ZB, LANES),
        panels.T,
        shapes.T,
    )


def emit_edges(q, inverse, pressure, up_ref, down_ref, right_ref, left_ref):
    row = lax.broadcasted_iota(jnp.int32, (YB, LANES), 0)
    even = row % 2 == 0
    normal = flux(q, pressure, inverse, 1)
    for f in range(5):
        for zq in range(4):
            top = bottom = None
            for z4 in range(4):
                plane = normal[f][zq * 4 + z4]
                last = turn(plane, 2 * z4 + 2)
                head = turn(plane, 2 * z4)
                mine = (row >= 2 * z4) & (row < 2 * z4 + 2)
                top = last if top is None else jnp.where(mine, last, top)
                bottom = head if bottom is None else jnp.where(mine, head, bottom)
            up_ref[f, zq] = far * top - jnp.where(even, near * turn(top, -1), 0.0)
            bottom = jnp.where(even, 0.0, near * turn(bottom, 1)) - far * bottom
            down_ref[f, zq] = turn(bottom, 6)
    ends = [q[f][0:2] for f in range(5)], [q[f][14:16] for f in range(5)]
    low = flux(ends[0], pressure[0:2], inverse[0:2], 2)
    high = flux(ends[1], pressure[14:16], inverse[14:16], 2)
    for f in range(5):
        left_ref[f, 0] = -far * low[f][0]
        left_ref[f, 1] = near * low[f][0] - far * low[f][1]
        right_ref[f, 0] = far * high[f][0] - near * high[f][1]
        right_ref[f, 1] = far * high[f][1]


edge_shapes = [shaped(5, 4, YB, 1024)] * 2 + [shaped(5, 2, YB, 1024)] * 2
STEPS = 2
STRIP = 1024 // STEPS
PARTS = STRIP // LANES
yedge_spec = pl.BlockSpec((5, 4, YB, STRIP), lambda s: (0, 0, 0, s))
zedge_spec = pl.BlockSpec((5, 2, YB, STRIP), lambda s: (0, 0, 0, s))
edge_specs = [yedge_spec] * 2 + [zedge_spec] * 2
line_spec = pl.BlockSpec((5, ZB, YB, STRIP), lambda s: (0, 0, 0, s))
cell_spec = pl.BlockSpec((ZB, YB, STRIP), lambda s: (0, 0, s))
code_spec = pl.BlockSpec((ZB, STRIP), lambda s: (0, s))


def by_lanes(kernel, packed_at=None):
    def run(*refs):
        for c in range(PARTS):
            lanes = pl.ds(c * LANES, LANES)
            views = []
            for i, ref in enumerate(refs):
                if i == packed_at:
                    views.append(ref.at[pl.ds(2 * c, 2)])
                else:
                    views.append(ref.at[(slice(None),) * (len(ref.shape) - 1) + (lanes,)])
            kernel(*views)

    return run


def missing(f, z, up_ref, down_ref, right_ref, left_ref):
    row = lax.broadcasted_iota(jnp.int32, (YB, LANES), 0)
    zq, z4 = z // 4, z % 4
    mine = (row >= 2 * z4) & (row < 2 * z4 + 2)
    both = turn(jnp.where(mine, up_ref[f, zq], down_ref[f, zq]), -2 * z4)
    value = jnp.where((row < 2) | (row > 5), both, 0.0)
    if z < 2:
        value = value + right_ref[f, z]
    if z > 13:
        value = value + left_ref[f, z - 14]
    return value


def exchange(up, down, right, left):
    ahead = [(SNAKE[b], SNAKE[b + 1]) for b in range(15)]
    back = [(SNAKE[b + 1], SNAKE[b]) for b in range(15)]
    return (
        lax.ppermute(up, "gx", ahead),
        lax.ppermute(down, "gx", back),
        lax.ppermute(right, "gz", [(g, (g + 1) % 8) for g in range(8)]),
        lax.ppermute(left, "gz", [((g + 1) % 8, g) for g in range(8)]),
    )


def join(a, b):
    lane = lax.broadcasted_iota(jnp.int32, a.shape, a.ndim - 1)
    axis = a.ndim - 1
    low = jnp.where(lane < HALF, a, pltpu.roll(b, HALF, axis))
    high = jnp.where(lane < HALF, pltpu.roll(a, HALF, axis), b)
    return jnp.concatenate([low, high], axis=0)


def unpack_kernel(in_ref, line_ref, metric_ref, code_ref, *edges):
    q = []
    for f in range(5):
        field = join(in_ref[0, f * 8 : f * 8 + 8], in_ref[1, f * 8 : f * 8 + 8])
        line_ref[f] = field
        q.append(field)
    metric_ref[...] = join(in_ref[0, 40:48], in_ref[1, 40:48])
    code_ref[...] = join(in_ref[0, 48], in_ref[1, 48])
    inverse = 1.0 / q[0]
    emit_edges(q, inverse, pressure_of(q, inverse), *edges)


def unpack(packed):
    return pl.pallas_call(
        by_lanes(unpack_kernel, 0),
        grid=(STEPS,),
        out_shape=[shaped(5, ZB, YB, 1024), shaped(ZB, YB, 1024), shaped(ZB, 1024), *edge_shapes],
        in_specs=[pl.BlockSpec((2 * PARTS, 49, YB, LANES), lambda s: (s, 0, 0, 0))],
        out_specs=[line_spec, cell_spec, code_spec, *edge_specs],
        compiler_params=grant(16),
        cost_estimate=cost(10000000, 8000000),
        name="unpack",
    )(packed)


def inner_slopes(q, f, normal, span):
    row = lax.broadcasted_iota(jnp.int32, (YB, LANES), 0)
    rows = []
    for z in range(ZB):
        g = normal[f][z]
        back1 = jnp.where(row < 1, 0.0, turn(g, 1))
        back2 = jnp.where(row < 2, 0.0, turn(g, 2))
        ahead1 = jnp.where(row > 6, 0.0, turn(g, -1))
        ahead2 = jnp.where(row > 5, 0.0, turn(g, -2))
        slope = near * (ahead1 - back1) - far * (ahead2 - back2)
        for offset, weight in ((1, near), (-1, -near), (2, -far), (-2, far)):
            if 0 <= z + offset < ZB:
                slope = slope + weight * span[f][z + offset]
        rows.append(slope)
    return jnp.stack(rows)


WIDE = 256


def inner_kernel(second, *refs):
    if second:
        whole_ref, base_ref, metric_ref, d_ref, s_ref, out_ref, q_ref, fhi_ref, flo_ref, slope_ref, x_ref = refs
    else:
        whole_ref, metric_ref, d_ref, s_ref, out_ref, q_ref, fhi_ref, flo_ref, slope_ref, x_ref = refs
    step = pl.program_id(0)

    @pl.when(step == 0)
    def prepare():
        def part(s, carry):
            lanes = pl.ds(pl.multiple_of(s * LANES, LANES), LANES)
            q = [whole_ref[f, :, :, lanes] for f in range(5)]
            inverse = 1.0 / q[0]
            stream = flux(q, pressure_of(q, inverse), inverse, 0)
            for f in range(5):
                rows = pl.ds(f * 128, 128)
                q_ref[rows, lanes] = (q[f] - middle[f]).reshape(128, LANES).astype(bf16)
                value = stream[f].reshape(128, LANES)
                high = value.astype(bf16)
                fhi_ref[rows, lanes] = high
                flo_ref[rows, lanes] = (value - high.astype(f32)).astype(bf16)
            return carry

        lax.fori_loop(0, 8, part, 0)

    wide = pl.ds(pl.multiple_of(step * WIDE, WIDE), WIDE)
    for c in range(WIDE // LANES):
        lanes = pl.ds(pl.multiple_of(step * WIDE + c * LANES, LANES), LANES)
        q = [whole_ref[f, :, :, lanes] for f in range(5)]
        inverse = 1.0 / q[0]
        pressure = pressure_of(q, inverse)
        normal = flux(q, pressure, inverse, 1)
        span = flux(q, pressure, inverse, 2)
        for f in range(5):
            slope_ref[f, :, :, c * LANES : c * LANES + LANES] = inner_slopes(q, f, normal, span)

    dot = functools.partial(
        lax.dot_general,
        dimension_numbers=(((1,), (1,)), ((), ())),
        preferred_element_type=f32,
    )
    deriv = d_ref[wide, :]
    dhi = deriv.astype(bf16)
    dlo = (deriv - dhi.astype(f32)).astype(bf16)
    smooth = s_ref[wide, :]
    shi = smooth.astype(bf16)
    slo = (smooth - shi.astype(f32)).astype(bf16)
    ones = jnp.ones((16, 1024), bf16)
    sums = (dot(ones, shi) + dot(ones, slo))[0:1]
    fhi = fhi_ref[...]
    stream = dot(q_ref[...], shi) - (dot(fhi, dhi) + dot(flo_ref[...], dhi) + dot(fhi, dlo))
    for f in range(5):
        part = stream[f * 128 : f * 128 + 128]
        part = part + middle[f] * sums if middle[f] else part
        x_ref[f] = part.reshape(ZB, YB, WIDE)

    for f in range(5):
        scale = time_step * metric_ref[:, :, wide]
        value = whole_ref[f, :, :, wide] + scale * (x_ref[f] - slope_ref[f])
        if second:
            value = 0.5 * base_ref[f, :, :, wide] + 0.5 * value
        out_ref[f, :, :, wide] = value


def inner(state, metric, deriv, smooth, base=None):
    second = base is not None
    whole = pl.BlockSpec(memory_space=pltpu.VMEM)
    return pl.pallas_call(
        functools.partial(inner_kernel, second),
        grid=(1024 // WIDE,),
        out_shape=shaped(5, ZB, YB, 1024),
        in_specs=[whole] * (5 if second else 4),
        out_specs=whole,
        scratch_shapes=[pltpu.VMEM((640, 1024), bf16)] * 3 + [pltpu.VMEM((5, ZB, YB, WIDE), f32)] * 2,
        compiler_params=grant(26),
        cost_estimate=cost(8 * 640 * 1024 * 1024, 14000000),
        name="inner2" if second else "inner1",
    )(state, *([base] if second else []), metric, deriv, smooth)


def first_kernel(part_ref, metric_ref, up, down, right, left, out_ref, *edges):
    scale = time_step * metric_ref[...]
    new = []
    for f in range(5):
        halo = jnp.stack([missing(f, z, up, down, right, left) for z in range(ZB)])
        value = part_ref[f] - scale * halo
        out_ref[f] = value
        new.append(value)
    inverse = 1.0 / new[0]
    emit_edges(new, inverse, pressure_of(new, inverse), *edges)


def first_section(part, metric, halos):
    return pl.pallas_call(
        by_lanes(first_kernel),
        grid=(STEPS,),
        out_shape=[shaped(5, ZB, YB, 1024), *edge_shapes],
        in_specs=[line_spec, cell_spec, *edge_specs],
        out_specs=[line_spec, *edge_specs],
        compiler_params=grant(16),
        cost_estimate=cost(10000000, 9000000),
        name="first",
    )(part, metric, *halos)


def final_kernel(part_ref, metric_ref, up, down, right, left, out_ref, load_ref):
    metric = metric_ref[...]
    scale = (0.5 * time_step) * metric
    lane = lax.broadcasted_iota(jnp.int32, (8, YB, LANES), 2)
    final = []
    for f in range(5):
        halo = jnp.stack([missing(f, z, up, down, right, left) for z in range(ZB)])
        value = part_ref[f] - scale * halo
        final.append(value)
        low, high = value[0:8], value[8:16]
        out_ref[0, f * 8 : f * 8 + 8] = jnp.where(lane < HALF, low, pltpu.roll(high, HALF, 2))
        out_ref[1, f * 8 : f * 8 + 8] = jnp.where(lane < HALF, pltpu.roll(low, HALF, 2), high)
    load_ref[...] = (pressure_of(final, 1.0 / final[0]) - pressure_ref) * metric


def final_section(part, metric, halos):
    return pl.pallas_call(
        by_lanes(final_kernel, 6),
        grid=(STEPS,),
        out_shape=[pltpu.HBM((16, 40, YB, LANES), f32), shaped(ZB, YB, 1024)],
        in_specs=[line_spec, cell_spec, *edge_specs],
        out_specs=[pl.BlockSpec((2 * PARTS, 40, YB, LANES), lambda s: (s, 0, 0, 0)), cell_spec],
        compiler_params=grant(16),
        cost_estimate=cost(10000000, 9000000),
        name="final",
    )(part, metric, *halos)


def home_kernel(in_ref, d_hbm, m_hbm, e_hbm, flat, sem):
    targets = [d_hbm, m_hbm.at[0], m_hbm.at[1], m_hbm.at[2], e_hbm]
    stores = []
    for f in range(5):
        for zp in range(8):
            tile = jnp.concatenate([in_ref[SNAKE[b], f * 8 + zp] for b in range(16)], axis=0).T
            flat[f, pl.ds(zp, XB, stride=ZB), :] = tile[0:HALF]
            flat[f, pl.ds(zp + 8, XB, stride=ZB), :] = tile[HALF:LANES]
        store = pltpu.make_async_copy(flat.at[f], targets[f], sem.at[f])
        store.start()
        stores.append(store)
    for store in stores:
        store.wait()


def home(packed):
    vm = pl.BlockSpec(memory_space=pltpu.VMEM)
    hbm = pl.BlockSpec(memory_space=pl.ANY)
    d, m, e = pl.pallas_call(
        home_kernel,
        out_shape=[shaped(XB * ZB, LANES), shaped(3, XB * ZB, LANES), shaped(XB * ZB, LANES)],
        in_specs=[vm],
        out_specs=[hbm] * 3,
        scratch_shapes=[pltpu.VMEM((5, XB * ZB, LANES), f32), pltpu.SemaphoreType.DMA((5,))],
        compiler_params=grant(16),
        cost_estimate=cost(1000000, 5300000),
        name="home",
    )(packed)
    return (
        d.reshape(XB, ZB, LANES),
        m.reshape(3, XB, ZB, LANES),
        e.reshape(XB, ZB, LANES),
    )


def forces_kernel(load_ref, code_ref, table_ref, out_ref, sum_ref):
    sum_ref[...] = jnp.zeros_like(sum_ref)
    run_row = lax.broadcasted_iota(jnp.int32, (8, 1024), 0)
    shape_row = lax.broadcasted_iota(jnp.int32, (NSHAPE, 1024), 0).astype(f32).astype(bf16)
    one = jnp.ones((NSHAPE, 1024), bf16)
    none = jnp.zeros((NSHAPE, 1024), bf16)

    def step(z, carry):
        load = load_ref[z, pl.ds(0, 1), :]
        code = code_ref[pl.ds(z, 1), :].astype(jnp.int32)
        across = code[:, 0:1] >> 11
        along = (code >> 8) & 7
        shape = (code & 255).astype(f32).astype(bf16)
        hit = jnp.where(run_row == along, load, 0.0)
        high = hit.astype(bf16)
        low = (hit - high.astype(f32)).astype(bf16)
        shape_hits = jnp.where(shape_row == shape, one, none)
        both = lax.dot_general(
            jnp.concatenate([high, low], axis=0),
            shape_hits,
            (((1,), (1,)), ((), ())),
            preferred_element_type=f32,
        )
        both = both[0:8] + both[8:16]
        for r in range(8):
            sum_ref[r * 8 : r * 8 + 8] += jnp.where(across == r, both, 0.0)
        return carry

    lax.fori_loop(0, ZB, step, 0)
    out_ref[...] = jnp.dot(
        sum_ref[...], table_ref[...], precision=lax.Precision.HIGHEST, preferred_element_type=f32
    )


def forces(load, code, table):
    vm = pl.BlockSpec(memory_space=pltpu.VMEM)
    return pl.pallas_call(
        forces_kernel,
        out_shape=shaped(NP, LANES),
        in_specs=[vm] * 3,
        out_specs=vm,
        scratch_shapes=[pltpu.VMEM((NP, NSHAPE), f32)],
        compiler_params=grant(16),
        cost_estimate=cost(2 * 16 * 256 * 16384, 700000),
        name="forces",
    )(load, code, table)


def spread_forces(held):
    for bit in (1, 2, 4):
        held = held + lax.ppermute(held, "gz", [(g, g ^ bit) for g in range(8)])
    me = lax.axis_index("gx")
    bit = 8
    while bit:
        half = held.shape[0] // 2
        got = lax.ppermute(held[half:], "gx", [(g, g + bit) for g in range(0, 16, 2 * bit)])
        held = jnp.where((me & bit) != 0, got, held[:half])
        bit //= 2
    return held


def body(
    density,
    momentum,
    energy,
    metric,
    deriv_matrix,
    smooth_matrix,
    panel_of_cell,
    shape_index,
    mode_table,
):
    outgoing = pack(density, momentum, energy, metric, panel_of_cell, shape_index)
    packed = lax.all_to_all(outgoing, "gx", split_axis=0, concat_axis=0, tiled=True)
    state, cells, code, *edges = unpack(packed)
    halos = exchange(*edges)
    part = inner(state, cells, deriv_matrix, smooth_matrix)
    first, *edges = first_section(part, cells, halos)
    halos = exchange(*edges)
    part = inner(first, cells, deriv_matrix, smooth_matrix, base=state)
    returning, load = final_section(part, cells, halos)
    packed = lax.all_to_all(returning, "gx", split_axis=0, concat_axis=0, tiled=True)
    panel_forces = spread_forces(forces(load, code, mode_table))
    new_density, new_momentum, new_energy = home(packed)
    return new_density, new_momentum, new_energy, panel_forces


def solution(mesh):
    in_specs = (
        P("gx", "gz", None),
        P(None, "gx", "gz", None),
        P("gx", "gz", None),
        P("gx", "gz", None),
        P(),
        P(),
        P("gx", "gz"),
        P("gx", "gz"),
        P(),
    )
    out_specs = (P("gx", "gz", None), P(None, "gx", "gz", None), P("gx", "gz", None), P("gx", None))
    return jax.shard_map(body, mesh=mesh, in_specs=in_specs, out_specs=out_specs, check_vma=False)
```

```python
import functools

import jax
import jax.numpy as jnp
from jax import lax
from jax.experimental import pallas as pl
from jax.experimental.pallas import tpu as pltpu
from jax.sharding import PartitionSpec as P

NP = 64
NSHAPE = 256
XB = 64
ZB = 16
YB = 8
LANES = 128
HALF = 64

time_step = 0.05
gas_factor = 0.4
pressure_ref = 2.0
middle = (1.5, 0.0, 0.0, 0.0, 5.0)
near = 8.0 / 12.0
far = 1.0 / 12.0

SNAKE = tuple(g if (g // 4) % 2 == 0 else 4 * (g // 4) + 3 - g % 4 for g in range(16))

f32 = jnp.float32
bf16 = jnp.bfloat16


def grant(mib):
    return pltpu.CompilerParams(vmem_limit_bytes=mib * 1024 * 1024)


def cost(flops, nbytes):
    return pl.CostEstimate(flops=flops, bytes_accessed=nbytes, transcendentals=0)


def shaped(*shape):
    return jax.ShapeDtypeStruct(shape, f32)


def pressure_of(q, inverse):
    return gas_factor * (q[4] - 0.5 * (q[1] * q[1] + q[2] * q[2] + q[3] * q[3]) * inverse)


def flux(q, pressure, inverse, direction):
    speed = q[1 + direction] * inverse
    parts = [q[1 + direction]]
    for component in range(3):
        term = q[1 + component] * speed
        if component == direction:
            term = term + pressure
        parts.append(term)
    parts.append((q[4] + pressure) * speed)
    return parts


def turn(v, shift):
    shift = shift % YB
    return pltpu.roll(v, shift, v.ndim - 2) if shift else v


def pack_kernel(
    d_hbm, m_hbm, e_hbm, g_hbm, panel_hbm, shape_hbm, out_hbm, raw, tiles, index, code_ref, in_sem, out_sem
):
    sources = [d_hbm, m_hbm.at[0], m_hbm.at[1], m_hbm.at[2], e_hbm, g_hbm]
    loads = [pltpu.make_async_copy(sources[f], raw.at[f], in_sem.at[f]) for f in range(6)]
    loads += [
        pltpu.make_async_copy(panel_hbm, index.at[0], in_sem.at[6]),
        pltpu.make_async_copy(shape_hbm, index.at[1], in_sem.at[7]),
    ]
    for load in loads:
        load.start()
    stores = []
    for f in range(6):
        if f == 5:
            loads[6].wait()
            loads[7].wait()
            turned = (index[0] * NSHAPE + index[1]).astype(f32)
            for peer in range(16):
                code_ref[peer, :, 0:HALF] = turned[0:8]
                code_ref[peer, :, HALF:LANES] = turned[8:16]
            store = pltpu.make_async_copy(code_ref, out_hbm.at[:, 48], out_sem.at[6])
            store.start()
            stores.append(store)
        loads[f].wait()
        for zp in range(8):
            low = raw[f, pl.ds(zp, XB, stride=ZB), :]
            high = raw[f, pl.ds(zp + 8, XB, stride=ZB), :]
            tile = jnp.concatenate([low, high], axis=0).T
            for peer in range(16):
                tiles[f, peer, zp] = tile[SNAKE[peer] * YB : SNAKE[peer] * YB + YB]
        store = pltpu.make_async_copy(tiles.at[f], out_hbm.at[:, f * 8 : f * 8 + 8], out_sem.at[f])
        store.start()
        stores.append(store)
    for store in stores:
        store.wait()


def pack(density, momentum, energy, metric, panels, shapes):
    hbm = pl.BlockSpec(memory_space=pl.ANY)
    return pl.pallas_call(
        pack_kernel,
        out_shape=shaped(16, 49, YB, LANES),
        in_specs=[hbm] * 6,
        out_specs=hbm,
        scratch_shapes=[
            pltpu.VMEM((6, XB * ZB, LANES), f32),
            pltpu.VMEM((6, 16, 8, YB, LANES), f32),
            pltpu.VMEM((2, ZB, XB), jnp.int32),
            pltpu.VMEM((16, YB, LANES), f32),
            pltpu.SemaphoreType.DMA((8,)),
            pltpu.SemaphoreType.DMA((7,)),
        ],
        compiler_params=pltpu.CompilerParams(),
        cost_estimate=cost(1000000, 6400000),
        name="pack",
    )(
        density.reshape(XB * ZB, LANES),
        momentum.reshape(3, XB * ZB, LANES),
        energy.reshape(XB * ZB, LANES),
        metric.reshape(XB * ZB, LANES),
        panels.T,
        shapes.T,
    )


def emit_edges(q, inverse, pressure, up_ref, down_ref, right_ref, left_ref):
    row = lax.broadcasted_iota(jnp.int32, (YB, LANES), 0)
    even = row % 2 == 0
    normal = flux(q, pressure, inverse, 1)
    for f in range(5):
        for zq in range(4):
            top = bottom = None
            for z4 in range(4):
                plane = normal[f][zq * 4 + z4]
                last = turn(plane, 2 * z4 + 2)
                head = turn(plane, 2 * z4)
                mine = (row >= 2 * z4) & (row < 2 * z4 + 2)
                top = last if top is None else jnp.where(mine, last, top)
                bottom = head if bottom is None else jnp.where(mine, head, bottom)
            up_ref[f, zq] = far * top - jnp.where(even, near * turn(top, -1), 0.0)
            bottom = jnp.where(even, 0.0, near * turn(bottom, 1)) - far * bottom
            down_ref[f, zq] = turn(bottom, 6)
    ends = [q[f][0:2] for f in range(5)], [q[f][14:16] for f in range(5)]
    low = flux(ends[0], pressure[0:2], inverse[0:2], 2)
    high = flux(ends[1], pressure[14:16], inverse[14:16], 2)
    for f in range(5):
        left_ref[f, 0] = -far * low[f][0]
        left_ref[f, 1] = near * low[f][0] - far * low[f][1]
        right_ref[f, 0] = far * high[f][0] - near * high[f][1]
        right_ref[f, 1] = far * high[f][1]


edge_shapes = [shaped(5, 4, YB, 1024)] * 2 + [shaped(5, 2, YB, 1024)] * 2
STEPS = 2
STRIP = 1024 // STEPS
PARTS = STRIP // LANES
in_place = pl.BlockSpec(memory_space=pltpu.VMEM)


def by_lanes(kernel, packed_at=None, blocked=False):
    def run(*refs):
        strip = pl.program_id(0)
        for c in range(PARTS):
            lanes = pl.ds(pl.multiple_of(strip * STRIP + c * LANES, LANES), LANES)
            peer = 2 * c if blocked else strip * (2 * PARTS) + 2 * c
            views = []
            for i, ref in enumerate(refs):
                if i == packed_at:
                    views.append(ref.at[pl.ds(peer, 2)])
                else:
                    views.append(ref.at[(slice(None),) * (len(ref.shape) - 1) + (lanes,)])
            kernel(*views)

    return run


def missing(f, z, up_ref, down_ref, right_ref, left_ref):
    row = lax.broadcasted_iota(jnp.int32, (YB, LANES), 0)
    zq, z4 = z // 4, z % 4
    mine = (row >= 2 * z4) & (row < 2 * z4 + 2)
    both = turn(jnp.where(mine, up_ref[f, zq], down_ref[f, zq]), -2 * z4)
    value = jnp.where((row < 2) | (row > 5), both, 0.0)
    if z < 2:
        value = value + right_ref[f, z]
    if z > 13:
        value = value + left_ref[f, z - 14]
    return value


def exchange(up, down, right, left):
    ahead = [(SNAKE[b], SNAKE[b + 1]) for b in range(15)]
    back = [(SNAKE[b + 1], SNAKE[b]) for b in range(15)]
    return (
        lax.ppermute(up, "gx", ahead),
        lax.ppermute(down, "gx", back),
        lax.ppermute(right, "gz", [(g, (g + 1) % 8) for g in range(8)]),
        lax.ppermute(left, "gz", [((g + 1) % 8, g) for g in range(8)]),
    )


def join(a, b):
    lane = lax.broadcasted_iota(jnp.int32, a.shape, a.ndim - 1)
    axis = a.ndim - 1
    low = jnp.where(lane < HALF, a, pltpu.roll(b, HALF, axis))
    high = jnp.where(lane < HALF, pltpu.roll(a, HALF, axis), b)
    return jnp.concatenate([low, high], axis=0)


def unpack_kernel(in_ref, line_ref, metric_ref, code_ref, *edges):
    q = []
    for f in range(5):
        field = join(in_ref[0, f * 8 : f * 8 + 8], in_ref[1, f * 8 : f * 8 + 8])
        line_ref[f] = field
        q.append(field)
    metric_ref[...] = join(in_ref[0, 40:48], in_ref[1, 40:48])
    code_ref[...] = join(in_ref[0, 48], in_ref[1, 48])
    inverse = 1.0 / q[0]
    emit_edges(q, inverse, pressure_of(q, inverse), *edges)


def unpack(packed):
    return pl.pallas_call(
        by_lanes(unpack_kernel, 0),
        grid=(STEPS,),
        out_shape=[shaped(5, ZB, YB, 1024), shaped(ZB, YB, 1024), shaped(ZB, 1024), *edge_shapes],
        in_specs=[in_place],
        out_specs=[in_place] * 7,
        compiler_params=grant(16),
        cost_estimate=cost(10000000, 8000000),
        name="unpack",
    )(packed)


def inner_slopes(q, f, normal, span):
    row = lax.broadcasted_iota(jnp.int32, (YB, LANES), 0)
    rows = []
    for z in range(ZB):
        g = normal[f][z]
        back1 = jnp.where(row < 1, 0.0, turn(g, 1))
        back2 = jnp.where(row < 2, 0.0, turn(g, 2))
        ahead1 = jnp.where(row > 6, 0.0, turn(g, -1))
        ahead2 = jnp.where(row > 5, 0.0, turn(g, -2))
        slope = near * (ahead1 - back1) - far * (ahead2 - back2)
        for offset, weight in ((1, near), (-1, -near), (2, -far), (-2, far)):
            if 0 <= z + offset < ZB:
                slope = slope + weight * span[f][z + offset]
        rows.append(slope)
    return jnp.stack(rows)


WIDE = 256


def inner_kernel(second, *refs):
    if second:
        whole_ref, base_ref, metric_ref, d_ref, s_ref, out_ref, q_ref, fhi_ref, flo_ref, slope_ref, x_ref = refs
    else:
        whole_ref, metric_ref, d_ref, s_ref, out_ref, q_ref, fhi_ref, flo_ref, slope_ref, x_ref = refs
    step = pl.program_id(0)

    @pl.when(step == 0)
    def prepare():
        def part(s, carry):
            lanes = pl.ds(pl.multiple_of(s * LANES, LANES), LANES)
            q = [whole_ref[f, :, :, lanes] for f in range(5)]
            inverse = 1.0 / q[0]
            stream = flux(q, pressure_of(q, inverse), inverse, 0)
            for f in range(5):
                rows = pl.ds(f * 128, 128)
                q_ref[rows, lanes] = (q[f] - middle[f]).reshape(128, LANES).astype(bf16)
                value = stream[f].reshape(128, LANES)
                high = value.astype(bf16)
                fhi_ref[rows, lanes] = high
                flo_ref[rows, lanes] = (value - high.astype(f32)).astype(bf16)
            return carry

        lax.fori_loop(0, 8, part, 0)

    wide = pl.ds(pl.multiple_of(step * WIDE, WIDE), WIDE)
    for c in range(WIDE // LANES):
        lanes = pl.ds(pl.multiple_of(step * WIDE + c * LANES, LANES), LANES)
        q = [whole_ref[f, :, :, lanes] for f in range(5)]
        inverse = 1.0 / q[0]
        pressure = pressure_of(q, inverse)
        normal = flux(q, pressure, inverse, 1)
        span = flux(q, pressure, inverse, 2)
        for f in range(5):
            slope_ref[f, :, :, c * LANES : c * LANES + LANES] = inner_slopes(q, f, normal, span)

    dot = functools.partial(
        lax.dot_general,
        dimension_numbers=(((1,), (1,)), ((), ())),
        preferred_element_type=f32,
    )
    deriv = d_ref[wide, :]
    dhi = deriv.astype(bf16)
    dlo = (deriv - dhi.astype(f32)).astype(bf16)
    smooth = s_ref[wide, :]
    shi = smooth.astype(bf16)
    slo = (smooth - shi.astype(f32)).astype(bf16)
    ones = jnp.ones((16, 1024), bf16)
    sums = (dot(ones, shi) + dot(ones, slo))[0:1]
    fhi = fhi_ref[...]
    stream = dot(q_ref[...], shi) - (dot(fhi, dhi) + dot(flo_ref[...], dhi) + dot(fhi, dlo))
    for f in range(5):
        part = stream[f * 128 : f * 128 + 128]
        part = part + middle[f] * sums if middle[f] else part
        x_ref[f] = part.reshape(ZB, YB, WIDE)

    for f in range(5):
        scale = time_step * metric_ref[:, :, wide]
        value = whole_ref[f, :, :, wide] + scale * (x_ref[f] - slope_ref[f])
        if second:
            value = 0.5 * base_ref[f, :, :, wide] + 0.5 * value
        out_ref[f, :, :, wide] = value


def inner(state, metric, deriv, smooth, base=None):
    second = base is not None
    whole = pl.BlockSpec(memory_space=pltpu.VMEM)
    return pl.pallas_call(
        functools.partial(inner_kernel, second),
        grid=(1024 // WIDE,),
        out_shape=shaped(5, ZB, YB, 1024),
        in_specs=[whole] * (5 if second else 4),
        out_specs=whole,
        scratch_shapes=[pltpu.VMEM((640, 1024), bf16)] * 3 + [pltpu.VMEM((5, ZB, YB, WIDE), f32)] * 2,
        compiler_params=grant(26),
        cost_estimate=cost(8 * 640 * 1024 * 1024, 14000000),
        name="inner2" if second else "inner1",
    )(state, *([base] if second else []), metric, deriv, smooth)


def first_kernel(part_ref, metric_ref, up, down, right, left, out_ref, *edges):
    scale = time_step * metric_ref[...]
    new = []
    for f in range(5):
        halo = jnp.stack([missing(f, z, up, down, right, left) for z in range(ZB)])
        value = part_ref[f] - scale * halo
        out_ref[f] = value
        new.append(value)
    inverse = 1.0 / new[0]
    emit_edges(new, inverse, pressure_of(new, inverse), *edges)


def first_section(part, metric, halos):
    return pl.pallas_call(
        by_lanes(first_kernel),
        grid=(STEPS,),
        out_shape=[shaped(5, ZB, YB, 1024), *edge_shapes],
        in_specs=[in_place] * 6,
        out_specs=[in_place] * 5,
        compiler_params=grant(16),
        cost_estimate=cost(10000000, 9000000),
        name="first",
    )(part, metric, *halos)


def final_kernel(part_ref, metric_ref, up, down, right, left, out_ref, load_ref):
    metric = metric_ref[...]
    scale = (0.5 * time_step) * metric
    lane = lax.broadcasted_iota(jnp.int32, (8, YB, LANES), 2)
    final = []
    for f in range(5):
        halo = jnp.stack([missing(f, z, up, down, right, left) for z in range(ZB)])
        value = part_ref[f] - scale * halo
        final.append(value)
        low, high = value[0:8], value[8:16]
        out_ref[0, f * 8 : f * 8 + 8] = jnp.where(lane < HALF, low, pltpu.roll(high, HALF, 2))
        out_ref[1, f * 8 : f * 8 + 8] = jnp.where(lane < HALF, pltpu.roll(low, HALF, 2), high)
    load_ref[...] = (pressure_of(final, 1.0 / final[0]) - pressure_ref) * metric


def final_section(part, metric, halos):
    return pl.pallas_call(
        by_lanes(final_kernel, 6, blocked=True),
        grid=(STEPS,),
        out_shape=[pltpu.HBM((16, 40, YB, LANES), f32), shaped(ZB, YB, 1024)],
        in_specs=[in_place] * 6,
        out_specs=[pl.BlockSpec((2 * PARTS, 40, YB, LANES), lambda s: (s, 0, 0, 0)), in_place],
        compiler_params=grant(16),
        cost_estimate=cost(10000000, 9000000),
        name="final",
    )(part, metric, *halos)


def home_kernel(in_ref, d_hbm, m_hbm, e_hbm, flat, sem):
    targets = [d_hbm, m_hbm.at[0], m_hbm.at[1], m_hbm.at[2], e_hbm]
    stores = []
    for f in range(5):
        for zp in range(8):
            tile = jnp.concatenate([in_ref[SNAKE[b], f * 8 + zp] for b in range(16)], axis=0).T
            flat[f, pl.ds(zp, XB, stride=ZB), :] = tile[0:HALF]
            flat[f, pl.ds(zp + 8, XB, stride=ZB), :] = tile[HALF:LANES]
        store = pltpu.make_async_copy(flat.at[f], targets[f], sem.at[f])
        store.start()
        stores.append(store)
    for store in stores:
        store.wait()


def home(packed):
    vm = pl.BlockSpec(memory_space=pltpu.VMEM)
    hbm = pl.BlockSpec(memory_space=pl.ANY)
    d, m, e = pl.pallas_call(
        home_kernel,
        out_shape=[shaped(XB * ZB, LANES), shaped(3, XB * ZB, LANES), shaped(XB * ZB, LANES)],
        in_specs=[vm],
        out_specs=[hbm] * 3,
        scratch_shapes=[pltpu.VMEM((5, XB * ZB, LANES), f32), pltpu.SemaphoreType.DMA((5,))],
        compiler_params=grant(16),
        cost_estimate=cost(1000000, 5300000),
        name="home",
    )(packed)
    return (
        d.reshape(XB, ZB, LANES),
        m.reshape(3, XB, ZB, LANES),
        e.reshape(XB, ZB, LANES),
    )


def forces_kernel(load_ref, code_ref, table_ref, out_ref, sum_ref):
    sum_ref[...] = jnp.zeros_like(sum_ref)
    run_row = lax.broadcasted_iota(jnp.int32, (8, 1024), 0)
    shape_row = lax.broadcasted_iota(jnp.int32, (NSHAPE, 1024), 0).astype(f32).astype(bf16)
    one = jnp.ones((NSHAPE, 1024), bf16)
    none = jnp.zeros((NSHAPE, 1024), bf16)

    def step(z, carry):
        load = load_ref[z, pl.ds(0, 1), :]
        code = code_ref[pl.ds(z, 1), :].astype(jnp.int32)
        across = code[:, 0:1] >> 11
        along = (code >> 8) & 7
        shape = (code & 255).astype(f32).astype(bf16)
        hit = jnp.where(run_row == along, load, 0.0)
        high = hit.astype(bf16)
        low = (hit - high.astype(f32)).astype(bf16)
        shape_hits = jnp.where(shape_row == shape, one, none)
        both = lax.dot_general(
            jnp.concatenate([high, low], axis=0),
            shape_hits,
            (((1,), (1,)), ((), ())),
            preferred_element_type=f32,
        )
        both = both[0:8] + both[8:16]
        for r in range(8):
            sum_ref[r * 8 : r * 8 + 8] += jnp.where(across == r, both, 0.0)
        return carry

    lax.fori_loop(0, ZB, step, 0)
    out_ref[...] = jnp.dot(
        sum_ref[...], table_ref[...], precision=lax.Precision.HIGHEST, preferred_element_type=f32
    )


def forces(load, code, table):
    vm = pl.BlockSpec(memory_space=pltpu.VMEM)
    return pl.pallas_call(
        forces_kernel,
        out_shape=shaped(NP, LANES),
        in_specs=[vm] * 3,
        out_specs=vm,
        scratch_shapes=[pltpu.VMEM((NP, NSHAPE), f32)],
        compiler_params=grant(16),
        cost_estimate=cost(2 * 16 * 256 * 16384, 700000),
        name="forces",
    )(load, code, table)


def spread_forces(held):
    for bit in (1, 2, 4):
        held = held + lax.ppermute(held, "gz", [(g, g ^ bit) for g in range(8)])
    me = lax.axis_index("gx")
    bit = 8
    while bit:
        half = held.shape[0] // 2
        got = lax.ppermute(held[half:], "gx", [(g, g + bit) for g in range(0, 16, 2 * bit)])
        held = jnp.where((me & bit) != 0, got, held[:half])
        bit //= 2
    return held


def body(
    density,
    momentum,
    energy,
    metric,
    deriv_matrix,
    smooth_matrix,
    panel_of_cell,
    shape_index,
    mode_table,
):
    outgoing = pack(density, momentum, energy, metric, panel_of_cell, shape_index)
    packed = lax.all_to_all(outgoing, "gx", split_axis=0, concat_axis=0, tiled=True)
    state, cells, code, *edges = unpack(packed)
    halos = exchange(*edges)
    part = inner(state, cells, deriv_matrix, smooth_matrix)
    first, *edges = first_section(part, cells, halos)
    halos = exchange(*edges)
    part = inner(first, cells, deriv_matrix, smooth_matrix, base=state)
    returning, load = final_section(part, cells, halos)
    packed = lax.all_to_all(returning, "gx", split_axis=0, concat_axis=0, tiled=True)
    panel_forces = spread_forces(forces(load, code, mode_table))
    new_density, new_momentum, new_energy = home(packed)
    return new_density, new_momentum, new_energy, panel_forces


def solution(mesh):
    in_specs = (
        P("gx", "gz", None),
        P(None, "gx", "gz", None),
        P("gx", "gz", None),
        P("gx", "gz", None),
        P(),
        P(),
        P("gx", "gz"),
        P("gx", "gz"),
        P(),
    )
    out_specs = (P("gx", "gz", None), P(None, "gx", "gz", None), P("gx", "gz", None), P("gx", None))
    return jax.shard_map(body, mesh=mesh, in_specs=in_specs, out_specs=out_specs, check_vma=False)
```

```python
import functools

import jax
import jax.numpy as jnp
from jax import lax
from jax.experimental import pallas as pl
from jax.experimental.pallas import tpu as pltpu
from jax.sharding import PartitionSpec as P

NP = 64
NSHAPE = 256
XB = 64
ZB = 16
YB = 8
LANES = 128
HALF = 64

time_step = 0.05
gas_factor = 0.4
pressure_ref = 2.0
middle = (1.5, 0.0, 0.0, 0.0, 5.0)
near = 8.0 / 12.0
far = 1.0 / 12.0

SNAKE = tuple(g if (g // 4) % 2 == 0 else 4 * (g // 4) + 3 - g % 4 for g in range(16))

f32 = jnp.float32
bf16 = jnp.bfloat16


def grant(mib):
    return pltpu.CompilerParams(vmem_limit_bytes=mib * 1024 * 1024)


def cost(flops, nbytes):
    return pl.CostEstimate(flops=flops, bytes_accessed=nbytes, transcendentals=0)


def shaped(*shape):
    return jax.ShapeDtypeStruct(shape, f32)


def pressure_of(q, inverse):
    return gas_factor * (q[4] - 0.5 * (q[1] * q[1] + q[2] * q[2] + q[3] * q[3]) * inverse)


def flux(q, pressure, inverse, direction):
    speed = q[1 + direction] * inverse
    parts = [q[1 + direction]]
    for component in range(3):
        term = q[1 + component] * speed
        if component == direction:
            term = term + pressure
        parts.append(term)
    parts.append((q[4] + pressure) * speed)
    return parts


def turn(v, shift):
    shift = shift % YB
    return pltpu.roll(v, shift, v.ndim - 2) if shift else v


def pack_kernel(
    d_hbm, m_hbm, e_hbm, g_hbm, panel_hbm, shape_hbm, out_hbm, raw, tiles, index, code_ref, in_sem, out_sem
):
    sources = [d_hbm, m_hbm.at[0], m_hbm.at[1], m_hbm.at[2], e_hbm, g_hbm]
    loads = [pltpu.make_async_copy(sources[f], raw.at[f], in_sem.at[f]) for f in range(6)]
    loads += [
        pltpu.make_async_copy(panel_hbm, index.at[0], in_sem.at[6]),
        pltpu.make_async_copy(shape_hbm, index.at[1], in_sem.at[7]),
    ]
    for load in loads:
        load.start()
    stores = []
    for f in range(6):
        if f == 5:
            loads[6].wait()
            loads[7].wait()
            turned = (index[0] * NSHAPE + index[1]).astype(f32)
            for peer in range(16):
                code_ref[peer, :, 0:HALF] = turned[0:8]
                code_ref[peer, :, HALF:LANES] = turned[8:16]
            store = pltpu.make_async_copy(code_ref, out_hbm.at[:, 48], out_sem.at[6])
            store.start()
            stores.append(store)
        loads[f].wait()
        for zp in range(8):
            low = raw[f, pl.ds(zp, XB, stride=ZB), :]
            high = raw[f, pl.ds(zp + 8, XB, stride=ZB), :]
            tile = jnp.concatenate([low, high], axis=0).T
            for peer in range(16):
                tiles[f, peer, zp] = tile[SNAKE[peer] * YB : SNAKE[peer] * YB + YB]
        store = pltpu.make_async_copy(tiles.at[f], out_hbm.at[:, f * 8 : f * 8 + 8], out_sem.at[f])
        store.start()
        stores.append(store)
    for store in stores:
        store.wait()


def pack(density, momentum, energy, metric, panels, shapes):
    hbm = pl.BlockSpec(memory_space=pl.ANY)
    return pl.pallas_call(
        pack_kernel,
        out_shape=shaped(16, 49, YB, LANES),
        in_specs=[hbm] * 6,
        out_specs=hbm,
        scratch_shapes=[
            pltpu.VMEM((6, XB * ZB, LANES), f32),
            pltpu.VMEM((6, 16, 8, YB, LANES), f32),
            pltpu.VMEM((2, ZB, XB), jnp.int32),
            pltpu.VMEM((16, YB, LANES), f32),
            pltpu.SemaphoreType.DMA((8,)),
            pltpu.SemaphoreType.DMA((7,)),
        ],
        compiler_params=pltpu.CompilerParams(),
        cost_estimate=cost(1000000, 6400000),
        name="pack",
    )(
        density.reshape(XB * ZB, LANES),
        momentum.reshape(3, XB * ZB, LANES),
        energy.reshape(XB * ZB, LANES),
        metric.reshape(XB * ZB, LANES),
        panels.T,
        shapes.T,
    )


def emit_edges(q, inverse, pressure, up_ref, down_ref, right_ref, left_ref):
    row = lax.broadcasted_iota(jnp.int32, (YB, LANES), 0)
    even = row % 2 == 0
    normal = flux(q, pressure, inverse, 1)
    for f in range(5):
        for zq in range(4):
            top = bottom = None
            for z4 in range(4):
                plane = normal[f][zq * 4 + z4]
                last = turn(plane, 2 * z4 + 2)
                head = turn(plane, 2 * z4)
                mine = (row >= 2 * z4) & (row < 2 * z4 + 2)
                top = last if top is None else jnp.where(mine, last, top)
                bottom = head if bottom is None else jnp.where(mine, head, bottom)
            up_ref[f, zq] = far * top - jnp.where(even, near * turn(top, -1), 0.0)
            bottom = jnp.where(even, 0.0, near * turn(bottom, 1)) - far * bottom
            down_ref[f, zq] = turn(bottom, 6)
    ends = [q[f][0:2] for f in range(5)], [q[f][14:16] for f in range(5)]
    low = flux(ends[0], pressure[0:2], inverse[0:2], 2)
    high = flux(ends[1], pressure[14:16], inverse[14:16], 2)
    for f in range(5):
        left_ref[f, 0] = -far * low[f][0]
        left_ref[f, 1] = near * low[f][0] - far * low[f][1]
        right_ref[f, 0] = far * high[f][0] - near * high[f][1]
        right_ref[f, 1] = far * high[f][1]


edge_shapes = [shaped(5, 4, YB, 1024)] * 2 + [shaped(5, 2, YB, 1024)] * 2
STEPS = 2
STRIP = 1024 // STEPS
PARTS = STRIP // LANES
in_place = pl.BlockSpec(memory_space=pltpu.VMEM)


def by_lanes(kernel, packed_at=None, blocked=False):
    def run(*refs):
        strip = pl.program_id(0)
        for c in range(PARTS):
            lanes = pl.ds(pl.multiple_of(strip * STRIP + c * LANES, LANES), LANES)
            peer = 2 * c if blocked else strip * (2 * PARTS) + 2 * c
            views = []
            for i, ref in enumerate(refs):
                if i == packed_at:
                    views.append(ref.at[pl.ds(peer, 2)])
                else:
                    views.append(ref.at[(slice(None),) * (len(ref.shape) - 1) + (lanes,)])
            kernel(*views)

    return run


def missing(f, z, up_ref, down_ref, right_ref, left_ref):
    row = lax.broadcasted_iota(jnp.int32, (YB, LANES), 0)
    zq, z4 = z // 4, z % 4
    mine = (row >= 2 * z4) & (row < 2 * z4 + 2)
    both = turn(jnp.where(mine, up_ref[f, zq], down_ref[f, zq]), -2 * z4)
    value = jnp.where((row < 2) | (row > 5), both, 0.0)
    if z < 2:
        value = value + right_ref[f, z]
    if z > 13:
        value = value + left_ref[f, z - 14]
    return value


def exchange(up, down, right, left):
    ahead = [(SNAKE[b], SNAKE[b + 1]) for b in range(15)]
    back = [(SNAKE[b + 1], SNAKE[b]) for b in range(15)]
    return (
        lax.ppermute(up, "gx", ahead),
        lax.ppermute(down, "gx", back),
        lax.ppermute(right, "gz", [(g, (g + 1) % 8) for g in range(8)]),
        lax.ppermute(left, "gz", [((g + 1) % 8, g) for g in range(8)]),
    )


def join(a, b):
    lane = lax.broadcasted_iota(jnp.int32, a.shape, a.ndim - 1)
    axis = a.ndim - 1
    low = jnp.where(lane < HALF, a, pltpu.roll(b, HALF, axis))
    high = jnp.where(lane < HALF, pltpu.roll(a, HALF, axis), b)
    return jnp.concatenate([low, high], axis=0)


def unpack_kernel(in_ref, line_ref, metric_ref, code_ref, *edges):
    q = []
    for f in range(5):
        field = join(in_ref[0, f * 8 : f * 8 + 8], in_ref[1, f * 8 : f * 8 + 8])
        line_ref[f] = field
        q.append(field)
    metric_ref[...] = join(in_ref[0, 40:48], in_ref[1, 40:48])
    code_ref[...] = join(in_ref[0, 48], in_ref[1, 48])
    inverse = 1.0 / q[0]
    emit_edges(q, inverse, pressure_of(q, inverse), *edges)


def unpack(packed):
    return pl.pallas_call(
        by_lanes(unpack_kernel, 0),
        grid=(STEPS,),
        out_shape=[shaped(5, ZB, YB, 1024), shaped(ZB, YB, 1024), shaped(ZB, 1024), *edge_shapes],
        in_specs=[in_place],
        out_specs=[in_place] * 7,
        compiler_params=grant(16),
        cost_estimate=cost(10000000, 8000000),
        name="unpack",
    )(packed)


def inner_slopes(q, f, normal, span):
    row = lax.broadcasted_iota(jnp.int32, (YB, LANES), 0)
    rows = []
    for z in range(ZB):
        g = normal[f][z]
        back1 = jnp.where(row < 1, 0.0, turn(g, 1))
        back2 = jnp.where(row < 2, 0.0, turn(g, 2))
        ahead1 = jnp.where(row > 6, 0.0, turn(g, -1))
        ahead2 = jnp.where(row > 5, 0.0, turn(g, -2))
        slope = near * (ahead1 - back1) - far * (ahead2 - back2)
        for offset, weight in ((1, near), (-1, -near), (2, -far), (-2, far)):
            if 0 <= z + offset < ZB:
                slope = slope + weight * span[f][z + offset]
        rows.append(slope)
    return jnp.stack(rows)


WIDE = 256


def inner_kernel(second, *refs):
    if second:
        whole_ref, base_ref, metric_ref, d_ref, s_ref, out_ref, q_ref, fhi_ref, flo_ref, slope_ref, x_ref = refs
    else:
        whole_ref, metric_ref, d_ref, s_ref, out_ref, q_ref, fhi_ref, flo_ref, slope_ref, x_ref = refs
    for s in range(8):
        lanes = slice(s * LANES, s * LANES + LANES)
        q = [whole_ref[f, :, :, lanes] for f in range(5)]
        inverse = 1.0 / q[0]
        stream = flux(q, pressure_of(q, inverse), inverse, 0)
        for f in range(5):
            rows = slice(f * 128, f * 128 + 128)
            q_ref[rows, lanes] = (q[f] - middle[f]).reshape(128, LANES).astype(bf16)
            value = stream[f].reshape(128, LANES)
            high = value.astype(bf16)
            fhi_ref[rows, lanes] = high
            flo_ref[rows, lanes] = (value - high.astype(f32)).astype(bf16)
    for step in range(1024 // WIDE):
        inner_strip(step, second, refs, slope_ref.at[step % 2], x_ref.at[step % 2])


def inner_strip(step, second, refs, slope_ref, x_ref):
    if second:
        whole_ref, base_ref, metric_ref, d_ref, s_ref, out_ref, q_ref, fhi_ref, flo_ref = refs[:9]
    else:
        whole_ref, metric_ref, d_ref, s_ref, out_ref, q_ref, fhi_ref, flo_ref = refs[:8]
    wide = slice(step * WIDE, step * WIDE + WIDE)
    for c in range(WIDE // LANES):
        lanes = slice(step * WIDE + c * LANES, step * WIDE + c * LANES + LANES)
        q = [whole_ref[f, :, :, lanes] for f in range(5)]
        inverse = 1.0 / q[0]
        pressure = pressure_of(q, inverse)
        normal = flux(q, pressure, inverse, 1)
        span = flux(q, pressure, inverse, 2)
        for f in range(5):
            slope_ref[f, :, :, c * LANES : c * LANES + LANES] = inner_slopes(q, f, normal, span)

    dot = functools.partial(
        lax.dot_general,
        dimension_numbers=(((1,), (1,)), ((), ())),
        preferred_element_type=f32,
    )
    deriv = d_ref[wide, :]
    dhi = deriv.astype(bf16)
    dlo = (deriv - dhi.astype(f32)).astype(bf16)
    smooth = s_ref[wide, :]
    shi = smooth.astype(bf16)
    slo = (smooth - shi.astype(f32)).astype(bf16)
    ones = jnp.ones((16, 1024), bf16)
    sums = (dot(ones, shi) + dot(ones, slo))[0:1]
    fhi = fhi_ref[...]
    stream = dot(q_ref[...], shi) - (dot(fhi, dhi) + dot(flo_ref[...], dhi) + dot(fhi, dlo))
    for f in range(5):
        part = stream[f * 128 : f * 128 + 128]
        part = part + middle[f] * sums if middle[f] else part
        x_ref[f] = part.reshape(ZB, YB, WIDE)

    for f in range(5):
        scale = time_step * metric_ref[:, :, wide]
        value = whole_ref[f, :, :, wide] + scale * (x_ref[f] - slope_ref[f])
        if second:
            value = 0.5 * base_ref[f, :, :, wide] + 0.5 * value
        out_ref[f, :, :, wide] = value


def inner(state, metric, deriv, smooth, base=None):
    second = base is not None
    whole = in_place
    return pl.pallas_call(
        functools.partial(inner_kernel, second),
        out_shape=shaped(5, ZB, YB, 1024),
        in_specs=[whole] * (5 if second else 4),
        out_specs=whole,
        scratch_shapes=[pltpu.VMEM((640, 1024), bf16)] * 3 + [pltpu.VMEM((2, 5, ZB, YB, WIDE), f32)] * 2,
        compiler_params=grant(26),
        cost_estimate=cost(8 * 640 * 1024 * 1024, 14000000),
        name="inner2" if second else "inner1",
    )(state, *([base] if second else []), metric, deriv, smooth)


def first_kernel(part_ref, metric_ref, up, down, right, left, out_ref, *edges):
    scale = time_step * metric_ref[...]
    new = []
    for f in range(5):
        halo = jnp.stack([missing(f, z, up, down, right, left) for z in range(ZB)])
        value = part_ref[f] - scale * halo
        out_ref[f] = value
        new.append(value)
    inverse = 1.0 / new[0]
    emit_edges(new, inverse, pressure_of(new, inverse), *edges)


def first_section(part, metric, halos):
    return pl.pallas_call(
        by_lanes(first_kernel),
        grid=(STEPS,),
        out_shape=[shaped(5, ZB, YB, 1024), *edge_shapes],
        in_specs=[in_place] * 6,
        out_specs=[in_place] * 5,
        compiler_params=grant(16),
        cost_estimate=cost(10000000, 9000000),
        name="first",
    )(part, metric, *halos)


def final_kernel(part_ref, metric_ref, up, down, right, left, out_ref, load_ref):
    metric = metric_ref[...]
    scale = (0.5 * time_step) * metric
    lane = lax.broadcasted_iota(jnp.int32, (8, YB, LANES), 2)
    final = []
    for f in range(5):
        halo = jnp.stack([missing(f, z, up, down, right, left) for z in range(ZB)])
        value = part_ref[f] - scale * halo
        final.append(value)
        low, high = value[0:8], value[8:16]
        out_ref[0, f * 8 : f * 8 + 8] = jnp.where(lane < HALF, low, pltpu.roll(high, HALF, 2))
        out_ref[1, f * 8 : f * 8 + 8] = jnp.where(lane < HALF, pltpu.roll(low, HALF, 2), high)
    load_ref[...] = (pressure_of(final, 1.0 / final[0]) - pressure_ref) * metric


def final_section(part, metric, halos):
    return pl.pallas_call(
        by_lanes(final_kernel, 6, blocked=True),
        grid=(STEPS,),
        out_shape=[pltpu.HBM((16, 40, YB, LANES), f32), shaped(ZB, YB, 1024)],
        in_specs=[in_place] * 6,
        out_specs=[pl.BlockSpec((2 * PARTS, 40, YB, LANES), lambda s: (s, 0, 0, 0)), in_place],
        compiler_params=grant(16),
        cost_estimate=cost(10000000, 9000000),
        name="final",
    )(part, metric, *halos)


def home_kernel(in_ref, d_hbm, m_hbm, e_hbm, flat, sem):
    targets = [d_hbm, m_hbm.at[0], m_hbm.at[1], m_hbm.at[2], e_hbm]
    stores = []
    for f in range(5):
        for zp in range(8):
            tile = jnp.concatenate([in_ref[SNAKE[b], f * 8 + zp] for b in range(16)], axis=0).T
            flat[f, pl.ds(zp, XB, stride=ZB), :] = tile[0:HALF]
            flat[f, pl.ds(zp + 8, XB, stride=ZB), :] = tile[HALF:LANES]
        store = pltpu.make_async_copy(flat.at[f], targets[f], sem.at[f])
        store.start()
        stores.append(store)
    for store in stores:
        store.wait()


def home(packed):
    vm = pl.BlockSpec(memory_space=pltpu.VMEM)
    hbm = pl.BlockSpec(memory_space=pl.ANY)
    d, m, e = pl.pallas_call(
        home_kernel,
        out_shape=[shaped(XB * ZB, LANES), shaped(3, XB * ZB, LANES), shaped(XB * ZB, LANES)],
        in_specs=[vm],
        out_specs=[hbm] * 3,
        scratch_shapes=[pltpu.VMEM((5, XB * ZB, LANES), f32), pltpu.SemaphoreType.DMA((5,))],
        compiler_params=grant(16),
        cost_estimate=cost(1000000, 5300000),
        name="home",
    )(packed)
    return (
        d.reshape(XB, ZB, LANES),
        m.reshape(3, XB, ZB, LANES),
        e.reshape(XB, ZB, LANES),
    )


def forces_kernel(load_ref, code_ref, table_ref, out_ref, sum_ref):
    sum_ref[...] = jnp.zeros_like(sum_ref)
    run_row = lax.broadcasted_iota(jnp.int32, (8, 1024), 0)
    shape_row = lax.broadcasted_iota(jnp.int32, (NSHAPE, 1024), 0).astype(f32).astype(bf16)
    one = jnp.ones((NSHAPE, 1024), bf16)
    none = jnp.zeros((NSHAPE, 1024), bf16)

    def step(z, carry):
        load = load_ref[z, pl.ds(0, 1), :]
        code = code_ref[pl.ds(z, 1), :].astype(jnp.int32)
        across = code[:, 0:1] >> 11
        along = (code >> 8) & 7
        shape = (code & 255).astype(f32).astype(bf16)
        hit = jnp.where(run_row == along, load, 0.0)
        high = hit.astype(bf16)
        low = (hit - high.astype(f32)).astype(bf16)
        shape_hits = jnp.where(shape_row == shape, one, none)
        both = lax.dot_general(
            jnp.concatenate([high, low], axis=0),
            shape_hits,
            (((1,), (1,)), ((), ())),
            preferred_element_type=f32,
        )
        both = both[0:8] + both[8:16]
        for r in range(8):
            sum_ref[r * 8 : r * 8 + 8] += jnp.where(across == r, both, 0.0)
        return carry

    lax.fori_loop(0, ZB, step, 0)
    out_ref[...] = jnp.dot(
        sum_ref[...], table_ref[...], precision=lax.Precision.HIGHEST, preferred_element_type=f32
    )


def forces(load, code, table):
    vm = pl.BlockSpec(memory_space=pltpu.VMEM)
    return pl.pallas_call(
        forces_kernel,
        out_shape=shaped(NP, LANES),
        in_specs=[vm] * 3,
        out_specs=vm,
        scratch_shapes=[pltpu.VMEM((NP, NSHAPE), f32)],
        compiler_params=grant(16),
        cost_estimate=cost(2 * 16 * 256 * 16384, 700000),
        name="forces",
    )(load, code, table)


def spread_forces(held):
    for bit in (1, 2, 4):
        held = held + lax.ppermute(held, "gz", [(g, g ^ bit) for g in range(8)])
    me = lax.axis_index("gx")
    bit = 8
    while bit:
        half = held.shape[0] // 2
        got = lax.ppermute(held[half:], "gx", [(g, g + bit) for g in range(0, 16, 2 * bit)])
        held = jnp.where((me & bit) != 0, got, held[:half])
        bit //= 2
    return held


def body(
    density,
    momentum,
    energy,
    metric,
    deriv_matrix,
    smooth_matrix,
    panel_of_cell,
    shape_index,
    mode_table,
):
    outgoing = pack(density, momentum, energy, metric, panel_of_cell, shape_index)
    packed = lax.all_to_all(outgoing, "gx", split_axis=0, concat_axis=0, tiled=True)
    state, cells, code, *edges = unpack(packed)
    halos = exchange(*edges)
    part = inner(state, cells, deriv_matrix, smooth_matrix)
    first, *edges = first_section(part, cells, halos)
    halos = exchange(*edges)
    part = inner(first, cells, deriv_matrix, smooth_matrix, base=state)
    returning, load = final_section(part, cells, halos)
    packed = lax.all_to_all(returning, "gx", split_axis=0, concat_axis=0, tiled=True)
    panel_forces = spread_forces(forces(load, code, mode_table))
    new_density, new_momentum, new_energy = home(packed)
    return new_density, new_momentum, new_energy, panel_forces


def solution(mesh):
    in_specs = (
        P("gx", "gz", None),
        P(None, "gx", "gz", None),
        P("gx", "gz", None),
        P("gx", "gz", None),
        P(),
        P(),
        P("gx", "gz"),
        P("gx", "gz"),
        P(),
    )
    out_specs = (P("gx", "gz", None), P(None, "gx", "gz", None), P("gx", "gz", None), P("gx", None))
    return jax.shard_map(body, mesh=mesh, in_specs=in_specs, out_specs=out_specs, check_vma=False)
```
